32 devices in a mesh: dp: 8 (over y, x, core), mp: 4 (over z).
Axes of the slice: x: 2, y: 2, z: 4, core: 2. Of those that a mesh axis runs over, the one named last changes fastest.
Arguments:
- tokens: bfloat16 [2048, 4096], P('dp'), may hold values from -6 to 6
- pack_source: int32 [2048], P('dp'), may hold values from 0 to 2047, as said below
- segment_ids: int32 [2048], P('dp'), may hold values from 0 to 3, never falling along the last dimension, each value on 1 to 1536 neighbouring positions
- w_in: bfloat16 [4096, 20480], P('dp', 'mp'), may hold values from -0.09375 to 0.09375
- w_dt: bfloat16 [4096, 128], P('dp', 'mp'), may hold values from -0.09375 to 0.09375
- w_out: bfloat16 [4096, 8192], P(None, 'mp'), may hold values from -0.0625 to 0.0625
- conv_x: float32 [4, 8192], P(None, 'mp'), may hold values from -3 to 3
- conv_bc: float32 [4, 2, 2048], P(None, None, 'mp'), may hold values from -3 to 3
- dt_bias: float32 [128], P('mp'), may hold values from -5 to -3
- decay_rate: float32 [128], P('mp'), may hold values from 0.0625 to 0.5
- skip_gain: float32 [128], P('mp'), may hold values from 0.1 to 0.5
- norm_gain: float32 [8192], P('mp'), may hold values from 0.1 to 1.9
Outputs:
- mixed: bfloat16 [2048, 4096], P(('dp', 'mp'))
The draws below stay inside these ranges and needn't reach their ends.
Inputs may be any that keep to these rules, and one draw needn't show every extreme that they name: pack_source is a permutation of the generation-order rows. Taking aligned blocks of 256 rows on both sides, a block of packed positions holds at most 64 rows of any one block of generation-order rows; each packed block holds exactly 64 rows of exactly one generation block, and each generation block gives exactly 64 rows to exactly one packed block. `segment_ids`: non-decreasing; each response has 1 to 1536 positions and one has exactly 1536.
All inputs are finite; a program needn't handle non-finite values.
Results may differ from the reference program's by a relative error of at most 0.012.
Values may be sent and summed in bfloat16 or wider, within the bound.
A program may use at most 192 MiB of HBM per device.

```python
import math
import jax
import jax.numpy as jnp
import numpy as np
from jax import lax

D = 4096
HEADS = 128
HEAD_DIM = 64
GROUPS = 8
STATE = 256
CONV = 4
BLOCK = 256
TOK_DEV = 256
DI = 8192
GN = 2048
PANEL = 5120
CAP = 64
TOKENS = 2048
SEGS = 4
SEG_MOST = 1536
N_DP = 8
N_MP = 4


def draw_pack_source(key, part):
    key_list = jax.random.split(jax.random.fold_in(key, 11), 6)
    device_count = N_DP
    row_total = TOK_DEV
    capacity = CAP
    lane_ids = jnp.arange(device_count, dtype=jnp.int32)
    peak_lane = jax.random.randint(key_list[0], (), 0, device_count)
    weights = jax.random.randint(key_list[1], (device_count,), 2, 4)
    weights = jnp.where(lane_ids == peak_lane, 0, weights).astype(jnp.int32)
    cum_weight = jnp.cumsum(weights).astype(jnp.int32)
    spread = (row_total - capacity) * cum_weight // cum_weight[-1]
    base_counts = spread - jnp.concatenate([jnp.zeros((1,), jnp.int32), spread[:-1]])
    base_counts = base_counts + capacity * (lane_ids == peak_lane).astype(jnp.int32)
    perm_source = jax.random.permutation(key_list[2], device_count)
    perm_target = jax.random.permutation(key_list[3], device_count)
    counts = base_counts[(perm_source[:, None] + perm_target[None, :]) % device_count]
    end_source = jnp.cumsum(counts, axis=1)
    start_source = end_source - counts
    start_target = jnp.cumsum(counts, axis=0) - counts
    positions = jnp.arange(row_total, dtype=jnp.int32)
    owner_dev = jnp.sum((positions[None, :, None] >= end_source[:, None, :]).astype(jnp.int32), axis=2)
    within = positions[None, :] - jnp.take_along_axis(start_source, owner_dev, axis=1)
    place_pre = jnp.take_along_axis(start_target, owner_dev, axis=1) + within
    source_perm = jax.vmap(lambda sub_key: jax.random.permutation(sub_key, row_total))(jax.random.split(key_list[4], device_count))
    target_perm = jax.vmap(lambda sub_key: jax.random.permutation(sub_key, row_total))(jax.random.split(key_list[5], device_count))
    slot_final = target_perm[owner_dev, place_pre]
    source_rows = lane_ids[:, None] * row_total + source_perm
    target_rows = owner_dev * row_total + slot_final
    packing = jnp.zeros((device_count * row_total,), jnp.int32).at[target_rows.reshape(-1)].set(source_rows.reshape(-1).astype(jnp.int32))
    return packing


def block_levels(own_key, extent, cuts, low, top_value):
    loudness, own = 1.0, jax.random.fold_in(own_key, 6)
    for axis_at, parts in cuts:
        steps = jnp.exp(jax.random.uniform(jax.random.fold_in(own, axis_at), (parts,), jnp.float32, low / len(cuts), top_value / len(cuts)))
        loudness = loudness * jnp.repeat(steps, extent[axis_at] // parts).reshape([-1 if axis == axis_at else 1 for axis in range(len(extent))])
    return loudness


def profile(amount, total, reach, skew):
    portions = [(1 << 20) // math.isqrt(grade ** skew) + 1 for grade in range(2, amount + 1)]
    rest, holding = total - reach - (amount - 1), [1] * (amount - 1)
    while rest > 0:
        free = [i for i in range(amount - 1) if holding[i] < reach]
        mass, remaining = sum([portions[i] for i in free]), rest
        for i in free:
            more = min(reach - holding[i], max(1, remaining * portions[i] // mass), rest)
            holding[i] = holding[i] + more
            rest = rest - more
    return np.array([reach] + holding)


def ragged(rng, number_of, total, reach, lean):
    if number_of == 2:
        one = jax.random.randint(rng, (), max(1, total - reach), min(reach, total - 1) + 1)
        return jnp.stack([one, total - one])
    sizes = jnp.asarray(profile(number_of, total, reach, lean), jnp.int32)
    couples = (number_of - 1) // 2
    donor, receiver = sizes[1:1 + 2 * couples:2], sizes[2:2 + 2 * couples:2]
    room = jnp.minimum(donor - 1, reach - receiver)
    moved = jax.random.randint(jax.random.fold_in(rng, 1), (couples,), 0, 1 << 20) % (room + 1)
    sizes = sizes.at[1:1 + 2 * couples:2].set(donor - moved).at[2:2 + 2 * couples:2].set(receiver + moved)
    return sizes[jax.random.permutation(jax.random.fold_in(rng, 2), number_of)]


def gaussian(rng, extent, scale, limit, cuts=(), kind=jnp.bfloat16):
    result = jax.random.normal(rng, extent, jnp.float32) * scale
    if len(cuts) > 0:
        result = block_levels(rng, extent, cuts, -0.22, 0.18) * result
    return jnp.clip(result, min=-limit, max=limit).astype(kind)


def setup_inputs(seed: int = 0) -> dict:
    streams_of = jax.random.split(jax.random.key(seed), 13)
    tokens = gaussian(streams_of[0], (TOKENS, D), 1.0, 6.0, ((0, 8),))
    pack_source = draw_pack_source(jax.random.fold_in(streams_of[12], 71), 0)
    segment_ids = jnp.searchsorted(jnp.cumsum(ragged(streams_of[2], SEGS, TOKENS, SEG_MOST, 1)), jnp.arange(TOKENS), side="right").astype(jnp.int32)
    w_in = gaussian(streams_of[3], (D, 2 * DI + 2 * GN), D ** -0.5, 0.09375, ((0, 8), (1, 4)))
    w_dt = gaussian(streams_of[4], (D, HEADS), D ** -0.5, 0.09375, ((0, 8), (1, 4)))
    w_out = gaussian(streams_of[5], (D, DI), DI ** -0.5, 0.0625, ((1, 4),))
    conv_x = gaussian(streams_of[6], (CONV, DI), 0.5, 3.0, ((1, 4),), jnp.float32)
    conv_bc = gaussian(streams_of[7], (CONV, 2, GN), 0.5, 3.0, ((2, 4),), jnp.float32)
    dt_bias = jnp.clip(-5.0 + 2.0 * jax.random.uniform(streams_of[8], (HEADS,), jnp.float32) ** block_levels(streams_of[8], (HEADS,), ((0, 4),), -0.2, 0.2), -5.0, -3.0)
    decay_rate = jnp.clip(jnp.exp(math.log(0.5) - 2.0794415 * jax.random.uniform(streams_of[9], (HEADS,), jnp.float32) ** block_levels(streams_of[9], (HEADS,), ((0, 4),), -0.2, 0.2)), 0.0625, 0.5)
    skip_gain = jnp.clip(0.1 + 0.4 * jax.random.uniform(streams_of[10], (HEADS,), jnp.float32) ** block_levels(streams_of[10], (HEADS,), ((0, 4),), -0.2, 0.2), 0.1, 0.5)
    norm_gain = jnp.clip(1.0 + 0.18 * jax.random.normal(streams_of[11], (DI,), jnp.float32), 0.1, 1.9)
    return dict(tokens=tokens, pack_source=pack_source, segment_ids=segment_ids, w_in=w_in, w_dt=w_dt, w_out=w_out, conv_x=conv_x, conv_bc=conv_bc, dt_bias=dt_bias, decay_rate=decay_rate, skip_gain=skip_gain, norm_gain=norm_gain)


highest = lax.Precision.HIGHEST

def block_step(carry, pieces):
    state_now, prev_seg = carry
    x_block, b_block, c_block, step_dt, step_rate, seg_block = pieces
    per_group = x_block.shape[1] // b_block.shape[1]
    cum_rate = jnp.cumsum(step_rate, axis=0)
    places = jnp.arange(seg_block.shape[0])
    linked = (seg_block[:, None] == seg_block[None, :]) & (places[:, None] >= places[None, :])
    log_spans = cum_rate.T[:, :, None] - cum_rate.T[:, None, :]
    decay_mat = jnp.where(linked[None], jnp.exp(jnp.where(linked[None], log_spans, 0.0)), 0.0)
    scores = jnp.einsum('tgn,sgn->gts', c_block.astype(jnp.float32), b_block.astype(jnp.float32), precision=highest)
    scores = jnp.repeat(scores, per_group, axis=0)
    mixing = (scores * decay_mat * step_dt.T[:, None, :]).astype(jnp.bfloat16)
    in_block = jnp.einsum('hts,shp->thp', mixing.astype(jnp.float32), x_block.astype(jnp.float32), precision=highest)
    c_heads = jnp.repeat(c_block.astype(jnp.float32), per_group, axis=1)
    b_heads = jnp.repeat(b_block.astype(jnp.float32), per_group, axis=1)
    entry_mask = jnp.where((seg_block == prev_seg)[:, None], jnp.exp(cum_rate), 0.0)
    from_before = entry_mask[:, :, None] * jnp.einsum('thn,hpn->thp', c_heads, state_now, precision=highest)
    last_seg = seg_block[-1]
    weight = jnp.where((seg_block == last_seg)[:, None], jnp.exp(cum_rate[-1][None, :] - cum_rate), 0.0) * step_dt
    carried = jnp.where(last_seg == prev_seg, jnp.exp(cum_rate[-1]), 0.0)
    added_in = jnp.einsum('shp,shn->hpn', weight[:, :, None] * x_block.astype(jnp.float32), b_heads, precision=highest)
    return ((carried[:, None, None] * state_now + added_in, last_seg), in_block + from_before)

def to_blocks(values):
    return values.reshape((TOKENS // BLOCK, BLOCK) + values.shape[1:])

def reference(tokens, pack_source, segment_ids, w_in, w_dt, w_out, conv_x, conv_bc, dt_bias, decay_rate, skip_gain, norm_gain):
    packed = tokens[pack_source]
    projected = jnp.dot(packed, w_in, preferred_element_type=jnp.float32).astype(jnp.bfloat16)
    panels = projected.reshape(TOKENS, N_MP, PANEL)
    chan_width = DI // N_MP
    group_width = GN // N_MP
    x_in = panels[:, :, :chan_width].reshape(TOKENS, DI)
    z_in = panels[:, :, chan_width:2 * chan_width].reshape(TOKENS, DI)
    b_in = panels[:, :, 2 * chan_width:2 * chan_width + group_width].reshape(TOKENS, GN)
    c_in = panels[:, :, 2 * chan_width + group_width:].reshape(TOKENS, GN)
    dt_raw = jnp.dot(packed, w_dt, preferred_element_type=jnp.float32)
    stacked = jnp.concatenate([x_in, b_in, c_in], axis=1)
    kernel = jnp.concatenate([conv_x, conv_bc.reshape(CONV, 2 * GN)], axis=1)
    extended = jnp.concatenate([jnp.zeros((CONV - 1, DI + 2 * GN), jnp.bfloat16), stacked], axis=0)
    seg_ext = jnp.concatenate([jnp.full((CONV - 1,), -1, jnp.int32), segment_ids], axis=0)
    conv_sum = jnp.zeros((TOKENS, DI + 2 * GN), jnp.float32)
    for lag_index in range(CONV):
        same_seg = (seg_ext[lag_index:lag_index + TOKENS] == segment_ids)[:, None]
        conv_sum = conv_sum + jnp.where(same_seg, kernel[lag_index][None, :] * extended[lag_index:lag_index + TOKENS].astype(jnp.float32), 0.0)
    convolved = jax.nn.silu(conv_sum).astype(jnp.bfloat16)
    x_all = convolved[:, :DI].reshape(TOKENS, HEADS, HEAD_DIM)
    b_all = convolved[:, DI:DI + GN].reshape(TOKENS, GROUPS, STATE)
    c_all = convolved[:, DI + GN:].reshape(TOKENS, GROUPS, STATE)
    step_dt = jax.nn.softplus(dt_raw + dt_bias)
    step_rate = -step_dt * decay_rate
    initial = (jnp.zeros((HEADS, HEAD_DIM, STATE), jnp.float32), jnp.array(-1, jnp.int32))
    final, outputs = lax.scan(block_step, initial, (to_blocks(x_all), to_blocks(b_all), to_blocks(c_all), to_blocks(step_dt), to_blocks(step_rate), to_blocks(segment_ids)))
    scan_out = outputs.reshape(TOKENS, HEADS, HEAD_DIM) + skip_gain[None, :, None] * x_all.astype(jnp.float32)
    gated_out = scan_out.reshape(TOKENS, DI) * jax.nn.silu(z_in.astype(jnp.float32))
    grouped = gated_out.reshape(TOKENS, GROUPS, DI // GROUPS)
    inv_rms = lax.rsqrt(lax.optimization_barrier(jnp.mean(grouped * grouped, axis=2, keepdims=True)) + 1e-05)
    normed = ((grouped * inv_rms).reshape(TOKENS, DI) * norm_gain).astype(jnp.bfloat16)

    def add_panel(accum, panel_index):
        first_col = panel_index * chan_width
        left_part = lax.dynamic_slice_in_dim(normed, first_col, chan_width, 1)
        right_part = lax.dynamic_slice_in_dim(w_out, first_col, chan_width, 1)
        partial_sum = lax.dot_general(left_part, right_part, (((1,), (1,)), ((), ())), preferred_element_type=jnp.float32).astype(jnp.bfloat16)
        partial_sum = lax.optimization_barrier(partial_sum).astype(jnp.float32)
        return (accum + partial_sum, None)
    accum, _ = lax.scan(add_panel, jnp.zeros((TOKENS, D), jnp.float32), jnp.arange(N_MP, dtype=jnp.int32))
    return accum.astype(jnp.bfloat16)
```

```python
import jax
import jax.numpy as jnp
from jax import lax
from jax.experimental import pallas as pl
from jax.experimental.pallas import tpu as pltpu
from jax.sharding import PartitionSpec as P

HEAD_DIM = 64
STATE = 256
CONV = 4
BLOCK = 256


highest = lax.Precision.HIGHEST


def passed_along(x, axis, by):
    size = lax.axis_size(axis)
    pairs = [(i, i + by) for i in range(size) if 0 <= i + by < size]
    return lax.ppermute(x, axis, pairs)


def carried_in(x, axis, join, neutral):
    place = lax.axis_index(axis)
    gathered = jax.tree.map(
        lambda a, kind: lax.all_gather(a.astype(kind), axis), x, (jnp.bfloat16, jnp.bfloat16)
    )
    state = jax.tree.map(lambda a, e: jnp.zeros_like(a) + jnp.asarray(e, a.dtype), x, neutral)

    def one(hop, state):
        return join(
            state,
            jax.tree.map(
                lambda a, own: lax.dynamic_index_in_dim(a, hop, 0, False).astype(own.dtype),
                gathered,
                x,
            ),
        )

    return lax.fori_loop(0, place, one, state)


def chain_combine(earlier, later_part):
    return (earlier[0] * later_part[0], later_part[0][:, None, None] * earlier[1] + later_part[1])


def running_sum(values):
    places = jnp.arange(values.shape[0])
    lower = (places[:, None] >= places[None, :]).astype(values.dtype)
    return jnp.dot(lower, values, precision=highest)


def block_step(carry, pieces):
    state_now, prev_seg = carry
    x_block, b_block, c_block, step_dt, step_rate, seg_block = pieces
    per_group = x_block.shape[1] // b_block.shape[1]
    cum_rate = running_sum(step_rate)
    places = jnp.arange(seg_block.shape[0])
    linked = (seg_block[:, None] == seg_block[None, :]) & (places[:, None] >= places[None, :])
    log_spans = cum_rate.T[:, :, None] - cum_rate.T[:, None, :]
    decay_mat = jnp.where(linked[None], jnp.exp(jnp.where(linked[None], log_spans, 0.0)), 0.0)
    scores = jnp.einsum("tgn,sgn->gts", c_block, b_block, preferred_element_type=jnp.float32)
    scores = jnp.repeat(scores, per_group, axis=0)
    mixing = (scores * decay_mat * step_dt.T[:, None, :]).astype(jnp.bfloat16)
    in_block = jnp.einsum("hts,shp->thp", mixing, x_block, preferred_element_type=jnp.float32)
    c_heads = jnp.repeat(c_block.astype(jnp.float32), per_group, axis=1)
    b_heads = jnp.repeat(b_block.astype(jnp.float32), per_group, axis=1)
    entry_mask = jnp.where((seg_block == prev_seg)[:, None], jnp.exp(cum_rate), 0.0)
    from_before = entry_mask[:, :, None] * jnp.einsum(
        "thn,hpn->thp", c_heads, state_now, precision=highest
    )
    last_seg = seg_block[-1]
    weight = (
        jnp.where((seg_block == last_seg)[:, None], jnp.exp(cum_rate[-1][None, :] - cum_rate), 0.0)
        * step_dt
    )
    carried = jnp.where(last_seg == prev_seg, jnp.exp(cum_rate[-1]), 0.0)
    added_in = jnp.einsum(
        "shp,shn->hpn", weight[:, :, None] * x_block.astype(jnp.float32), b_heads, precision=highest
    )
    return ((carried[:, None, None] * state_now + added_in, last_seg), in_block + from_before)


def on_device(
    tokens,
    pack_source,
    segment_ids,
    w_in,
    w_dt,
    w_out,
    conv_x,
    conv_bc,
    dt_bias,
    decay_rate,
    skip_gain,
    norm_gain,
):
    row_count = tokens.shape[0]
    data_devs = lax.axis_size("dp")
    capacity = 2 * row_count // data_devs
    source_dev = pack_source // row_count
    source_row = pack_source % row_count
    same_source = source_dev[:, None] == source_dev[None, :]
    earlier_rows = pack_source[None, :] < pack_source[:, None]
    rank_in = jnp.sum((same_source & earlier_rows).astype(jnp.int32), axis=1)
    slot_index = source_dev * capacity + rank_in
    requests = (
        jnp.full((data_devs * capacity,), -1, jnp.int32)
        .at[slot_index]
        .set(source_row)
        .reshape(data_devs, capacity)
    )
    wanted = lax.all_to_all(requests, "dp", split_axis=0, concat_axis=0, tiled=True)
    fetched = jnp.where(
        (wanted >= 0)[:, :, None], tokens[jnp.maximum(wanted, 0)], jnp.zeros((), jnp.bfloat16)
    )
    replies = lax.all_to_all(fetched, "dp", split_axis=0, concat_axis=0, tiled=True)
    gathered = replies.reshape(data_devs * capacity, tokens.shape[1])[slot_index]
    panel_cols = w_in.shape[1]
    head_count = w_dt.shape[1]
    chan_width = w_out.shape[1]
    proj_sum = jnp.dot(
        gathered, lax.all_gather(w_in, "dp", axis=0, tiled=True), preferred_element_type=jnp.float32
    )
    step_sum = jnp.dot(
        gathered, lax.all_gather(w_dt, "dp", axis=0, tiled=True), preferred_element_type=jnp.float32
    )
    proj_sum, dt_raw = (proj_sum, step_sum)
    projected = proj_sum.astype(jnp.bfloat16)
    group_width = (panel_cols - 2 * chan_width) // 2
    gate_in = projected[:, chan_width : 2 * chan_width]
    stacked = jnp.concatenate([projected[:, :chan_width], projected[:, 2 * chan_width :]], axis=1)
    tail_len = CONV - 1
    tail_vals = stacked[row_count - tail_len :].astype(jnp.float32)
    tail_seg = (segment_ids[row_count - tail_len :] + 1).astype(jnp.float32)
    prev_vals, prev_seg = passed_along((tail_vals, tail_seg), "dp", 1)
    extended = jnp.concatenate([prev_vals.astype(jnp.bfloat16), stacked], axis=0)
    seg_ext = jnp.concatenate([prev_seg.astype(jnp.int32) - 1, segment_ids], axis=0)
    kernel = jnp.concatenate([conv_x, conv_bc.reshape(CONV, 2 * group_width)], axis=1)
    conv_sum = jnp.zeros((row_count, stacked.shape[1]), jnp.float32)
    for lag_index in range(CONV):
        same_seg = (seg_ext[lag_index : lag_index + row_count] == segment_ids)[:, None]
        conv_sum = conv_sum + jnp.where(
            same_seg,
            kernel[lag_index][None, :]
            * extended[lag_index : lag_index + row_count].astype(jnp.float32),
            0.0,
        )
    convolved = jax.nn.silu(conv_sum).astype(jnp.bfloat16)
    local_groups = group_width // STATE
    x_all = convolved[:, :chan_width].reshape(row_count, head_count, HEAD_DIM)
    b_all = convolved[:, chan_width : chan_width + group_width].reshape(
        row_count, local_groups, STATE
    )
    c_all = convolved[:, chan_width + group_width :].reshape(row_count, local_groups, STATE)
    step_dt = jax.nn.softplus(dt_raw + dt_bias)
    step_rate = -step_dt * decay_rate
    seg_before = seg_ext[tail_len - 1]
    block_total = row_count // BLOCK

    def to_blocks(values):
        return values.reshape((block_total, BLOCK) + values.shape[1:])

    start_state = (jnp.zeros((head_count, HEAD_DIM, STATE), jnp.float32), seg_before)
    final, outputs = lax.scan(
        block_step,
        start_state,
        (
            to_blocks(x_all),
            to_blocks(b_all),
            to_blocks(c_all),
            to_blocks(step_dt),
            to_blocks(step_rate),
            to_blocks(segment_ids),
        ),
    )
    local_state = final[0]
    scan_out = outputs.reshape(row_count, head_count, HEAD_DIM)
    running = running_sum(step_rate)
    carry_gain = jnp.where(segment_ids[-1] == seg_before, jnp.exp(running[-1]), 0.0)
    neutral = (jnp.ones((head_count,), jnp.float32), jnp.zeros_like(local_state))
    incoming = carried_in((carry_gain, local_state), "dp", chain_combine, neutral)[1]
    c_heads = jnp.repeat(c_all.astype(jnp.float32), head_count // local_groups, axis=1)
    entry_mask = jnp.where((segment_ids == seg_before)[:, None], jnp.exp(running), 0.0)
    scan_out = scan_out + entry_mask[:, :, None] * jnp.einsum(
        "thn,hpn->thp", c_heads, incoming, precision=highest
    )
    scan_out = scan_out + skip_gain[None, :, None] * x_all.astype(jnp.float32)
    gated_out = scan_out.reshape(row_count, chan_width) * jax.nn.silu(gate_in.astype(jnp.float32))
    grouped = gated_out.reshape(row_count, local_groups, chan_width // local_groups)
    inv_rms = lax.rsqrt(jnp.mean(grouped * grouped, axis=2, keepdims=True) + 1e-05)
    normed = ((grouped * inv_rms).reshape(row_count, chan_width) * norm_gain).astype(jnp.bfloat16)
    return lax.psum_scatter(
        lax.dot_general(
            normed, w_out, (((1,), (1,)), ((), ())), preferred_element_type=jnp.float32
        ).astype(jnp.bfloat16),
        "mp",
        scatter_dimension=0,
        tiled=True,
    )


HALO = 16
CHUNKS = 4
MESH = pl.DeviceIdType.MESH


def remote(src, dst, send, recv, dp):
    return pltpu.make_async_remote_copy(
        src_ref=src, dst_ref=dst, send_sem=send, recv_sem=recv,
        device_id={"dp": dp}, device_id_type=MESH,
    )


def along_mp(src, dst, send, recv, mp):
    return pltpu.make_async_remote_copy(
        src_ref=src, dst_ref=dst, send_sem=send, recv_sem=recv,
        device_id={"mp": mp}, device_id_type=MESH,
    )


def column(row):
    return jnp.broadcast_to(row, (128, row.shape[1])).T


def aligned(start, size):
    return pl.ds(pl.multiple_of(start, 128), size)


def mixer_kernel(
    tok_hbm, source_ref, segment_ref, w_hbm, wdt_ref, tapx_ref, tapbc_ref, head_ref, skip_ref, chan_ref,
    whole, sums,
    meta_ref, metas, tokg, idxcol, onehot, packed, wbuf, wdtt, wdtc, sent, got, own,
    dt_sent, dt_got, dt_own, same, bc, bt, xs, scores, bias,
    cum_t, dt_t, w_t, entry_t, enter_t, gain_t, entering, leaving, arriving, ssd, gated_out, square, sum_sent,
    loc_sem, wloc_sem, meta_send, meta_recv, y_send, y_recv, x_send, x_recv, d_send, d_recv, z_send, z_recv,
    s_send, s_recv, w_send, w_recv, v_send, v_recv, p_send, p_recv, t_send, t_recv, q_send, q_recv,
    bc_send, bc_recv, st_send, st_recv, g_send, g_recv, n_send, n_recv,
):
    f32, bf = jnp.float32, jnp.bfloat16
    me, m = lax.axis_index("dp"), lax.axis_index("mp")
    core = me % 2
    at_x = (me // 2) % 2
    at_y = me // 4
    sibling = me + 1 - 2 * core
    beside = m + 1 - 2 * (m % 2)
    half = m % 2
    x_dev = [4 * at_y + 2 * (1 - at_x) + c for c in (core, 1 - core)]
    y_dev = [4 * (1 - at_y) + 2 * at_x + c for c in (core, 1 - core)]
    d_dev = [4 * (1 - at_y) + 2 * (1 - at_x) + c for c in (core, 1 - core)]
    cores = (core, 1 - core)

    rows, depth = tok_hbm.shape[0], w_hbm.shape[0]
    width = w_hbm.shape[1] // 5
    group, state = width, width // 4
    share = group // 2
    feats = 2 * depth
    kdim = 2 * feats
    span = 4 * rows
    ext = span + HALO
    part = rows // 2
    chunk = feats // CHUNKS
    block = rows

    barrier = pltpu.get_barrier_semaphore()
    for k in range(1, 8):
        pl.semaphore_signal(barrier, inc=1, device_id={"dp": (me + k) % 8}, device_id_type=MESH)
    pl.semaphore_signal(barrier, inc=1, device_id={"mp": beside}, device_id_type=MESH)
    meta_ref[...] = jnp.concatenate(
        [source_ref[...], segment_ref[...], jnp.zeros((6, rows), jnp.int32)], axis=0
    )

    def of_tile(x, c, t):
        if t == 0:
            return 4 * width + c * 2 * state + x * state
        return (0, 0, state, 2 * width, 2 * width + state)[t] + x * group + c * share

    kmine = pl.ds(pl.multiple_of(depth * (2 * at_x + core), depth), depth)
    wlocal = []
    for t in range(5):
        wlocal.append(
            pltpu.make_async_copy(
                w_hbm.at[:, aligned(of_tile(at_x, core, t), state)],
                wbuf.at[kmine, pl.ds(t * state, state)], wloc_sem.at[t],
            )
        )
    wlocal.append(pltpu.make_async_copy(wdt_ref.at[2 * at_x + core], wdtt.at[:, kmine], wloc_sem.at[5]))
    mine_rows = pl.ds(pl.multiple_of(me * rows, rows), rows)

    def features(y, c, f, size):
        return aligned(y * kdim + c * feats + f * chunk, size)

    local_tok = pltpu.make_async_copy(
        tok_hbm.at[:, features(at_y, core, 0, feats)], tokg.at[mine_rows], loc_sem.at[0]
    )
    local_tok.start()
    for c in wlocal:
        c.start()
    pl.semaphore_wait(barrier, 8)

    copies = []
    for k in range(1, 8):
        copies.append(
            remote(meta_ref, metas.at[me], meta_send.at[k - 1], meta_recv.at[k - 1], (me + k) % 8)
        )
    local_meta = pltpu.make_async_copy(meta_ref, metas.at[me], loc_sem.at[1])
    for c in copies + [local_meta]:
        c.start()

    def half_rows(dev, which):
        return pl.ds(pl.multiple_of(dev * rows + which * part, part), part)

    def all_rows(dev):
        return pl.ds(pl.multiple_of(dev * rows, rows), rows)

    def fcols(f):
        return pl.ds(f * chunk, chunk)

    by_y, by_x, by_d, by_z = [], [], [], []
    for f in range(CHUNKS):
        by_y.append([
            remote(
                tok_hbm.at[:, features(1 - at_y, cores[r], f, chunk)], tokg.at[all_rows(me), fcols(f)],
                y_send.at[r, f], y_recv.at[r, f], y_dev[r],
            )
            for r in range(2)
        ])
        by_x.append([
            remote(
                tok_hbm.at[pl.ds(pl.multiple_of(half * part, part), part),
                           features(at_y, cores[r], f, chunk)],
                tokg.at[half_rows(me, half), fcols(f)],
                x_send.at[r, f], x_recv.at[r, f], x_dev[r],
            )
            for r in range(2)
        ])
        by_d.append([
            remote(
                tokg.at[half_rows(y_dev[r], half), fcols(f)], tokg.at[half_rows(y_dev[r], half), fcols(f)],
                d_send.at[r, f], d_recv.at[r, f], x_dev[0],
            )
            for r in range(2)
        ])
        by_z.append([
            along_mp(
                tokg.at[half_rows(dev, half), fcols(f)], tokg.at[half_rows(dev, half), fcols(f)],
                z_send.at[i, f], z_recv.at[i, f], beside,
            )
            for i, dev in enumerate(x_dev + d_dev)
        ])
    for f in range(CHUNKS):
        for c in by_y[f] + by_x[f]:
            c.start()
    to_sibling = remote(
        tok_hbm.at[:, features(at_y, 1 - core, 0, feats)], tokg.at[mine_rows],
        s_send, s_recv, sibling,
    )
    to_sibling.start()
    wsib = []
    for t in range(5):
        wsib.append(
            remote(
                w_hbm.at[:, aligned(of_tile(at_x, 1 - core, t), state)],
                wbuf.at[kmine, pl.ds(t * state, state)], w_send.at[0, t], w_recv.at[0, t], sibling,
            )
        )
    wsib.append(
        remote(wdt_ref.at[2 * at_x + 1 - core], wdtt.at[:, kmine], w_send.at[0, 5], w_recv.at[0, 5], sibling)
    )
    for c in wsib:
        c.start()

    quarter = depth // 4
    wfirst = [
        [
            remote(
                w_hbm.at[pl.ds(q * quarter, quarter), aligned(of_tile(1 - at_x, cores[r], 0), state)],
                wbuf.at[pl.ds(pl.multiple_of(depth * (2 * at_x + core) + q * quarter, quarter), quarter),
                        pl.ds(0, state)],
                v_send.at[r, q], v_recv.at[r, q], x_dev[r],
            )
            for r in range(2)
        ]
        for q in range(4)
    ]
    wrest = [
        [
            remote(
                w_hbm.at[:, aligned(of_tile(1 - at_x, cores[r], t), state)],
                wbuf.at[kmine, pl.ds(t * state, state)],
                w_send.at[1 + r, t], w_recv.at[1 + r, t], x_dev[r],
            )
            for r in range(2)
        ]
        for t in range(1, 5)
    ]
    wstep = [
        remote(
            wdt_ref.at[2 * (1 - at_x) + cores[r]], wdtt.at[:, kmine],
            w_send.at[1 + r, 5], w_recv.at[1 + r, 5], x_dev[r],
        )
        for r in range(2)
    ]

    for c in copies:
        c.wait_recv()
    local_meta.wait()
    idxcol[0:HALO, :] = jnp.full((HALO, 128), -1, jnp.int32)
    for j in range(8):
        idxcol[HALO + j * rows : HALO + (j + 1) * rows, :] = column(metas[j, 0:1, :])
    lanes = lax.broadcasted_iota(jnp.int32, (ext, 128), 1)

    def choose(which):
        ids = idxcol[pl.ds(pl.multiple_of(which * span, span), ext), :]

        @pl.loop(0, 8 * rows // 128)
        def _(t):
            onehot[:, pl.ds(pl.multiple_of(t * 128, 128), 128)] = jnp.where(
                ids == lanes + t * 128, 1.0, 0.0
            ).astype(bf)

    def place(f):
        return pl.ds(pl.multiple_of(core * feats + f * chunk, 128), chunk)

    def swap(slot, f):
        there = packed.at[slot, :, place(f)]
        return remote(there, there, q_send.at[slot, f], q_recv.at[slot, f], sibling)

    def pack(slot, f):
        packed[slot, :, place(f)] = jnp.dot(
            onehot[...], tokg[:, fcols(f)], preferred_element_type=f32
        ).astype(bf)
        swap(slot, f).start()

    choose(1 - at_y)

    def y_stage(f):
        for r in range(2):
            by_y[f][r].wait_recv()
            by_d[f][r].start()

    def x_stage(f):
        for r in range(2):
            by_x[f][r].wait_recv()
            by_z[f][r].start()

    def d_stage(f):
        for r in range(2):
            by_d[f][r].wait_recv()
            by_z[f][2 + r].start()

    def z_stage(f):
        for c in by_z[f]:
            c.wait_recv()

    def w_stage(q):
        for c in wfirst[q]:
            c.start()

    y_stage(0)
    x_stage(0)
    w_stage(0)
    y_stage(1)
    d_stage(0)
    x_stage(1)
    w_stage(1)
    local_tok.wait()
    to_sibling.wait_recv()
    y_stage(2)
    d_stage(1)
    x_stage(2)
    w_stage(2)
    z_stage(0)
    pack(0, 0)
    y_stage(3)
    d_stage(2)
    x_stage(3)
    w_stage(3)
    for c in wstep:
        c.start()
    for pair in wrest:
        for c in pair:
            c.start()
    z_stage(1)
    pack(0, 1)
    d_stage(3)
    z_stage(2)
    pack(0, 2)
    z_stage(3)
    pack(0, 3)

    def product(slot, t):
        return jnp.dot(packed[slot], wbuf[:, pl.ds(t * state, state)], preferred_element_type=f32)

    def partial(t):
        return remote(sent.at[t], got.at[t], p_send.at[t], p_recv.at[t], y_dev[0])

    def theirs(t):
        sent[t] = product(0, t).astype(bf)
        partial(t).start()

    def ours(t):
        own[:, pl.ds(t * state, state)] = product(1, t)

    step_copy = remote(dt_sent, dt_got, t_send, t_recv, y_dev[0])

    wlocal[0].wait()
    wsib[0].wait_recv()
    for q in range(4):
        for c in wfirst[q]:
            c.wait_recv()
    for f in range(CHUNKS):
        swap(0, f).wait_recv()
    theirs(0)
    wlocal[5].wait()
    wsib[5].wait_recv()
    for c in wstep:
        c.wait_recv()
    wdtc[...] = jnp.concatenate(
        [wdtt[...].astype(f32), jnp.zeros((112, kdim), f32)], axis=0
    ).T.astype(bf)
    dt_sent[...] = jnp.dot(packed[0, HALO:, :], wdtc[...], preferred_element_type=f32).T[0:8]
    step_copy.start()

    choose(at_y)
    for f in range(CHUNKS):
        pack(1, f)

    def seg_row(k):
        return metas[4 * at_y + k, 1:2, :]

    earlier = metas[(4 * at_y + 7) % 8, 1:2, :] * at_y - (1 - at_y)
    seg_ext = jnp.concatenate(
        [column(earlier)[rows - HALO :]] + [column(seg_row(k)) for k in range(4)], axis=0
    )
    for k in range(1, CONV):
        same[k - 1] = jnp.where(pltpu.roll(seg_ext, k, 0) == seg_ext, 1.0, 0.0)
    for k in range(4):
        seg_col = column(seg_row(k))
        for t in range(2):
            here = slice(t * 128, (t + 1) * 128)
            linked = (seg_col == seg_row(k)[:, here]) & (
                lax.broadcasted_iota(jnp.int32, (block, 128), 0)
                >= lax.broadcasted_iota(jnp.int32, (block, 128), 1) + t * 128
            )
            bias[k, :, here] = jnp.where(linked, 0.0, -1e30)

    for f in range(CHUNKS):
        swap(1, f).wait_recv()
    ours(0)
    dt_own[...] = jnp.dot(packed[1, HALO:, :], wdtc[...], preferred_element_type=f32).T[0:8]

    def next_tile(t):
        wlocal[t].wait()
        wsib[t].wait_recv()
        for c in wrest[t - 1]:
            c.wait_recv()
        theirs(t)
        ours(t)

    def projected(k, col, size):
        at = pl.ds(k * block, size)
        t, off = col // state, col % state
        total = own[at, pl.ds(col, 128)] + got[t, at, pl.ds(off, 128)].astype(f32)
        return total.astype(bf).astype(f32)

    def convolved(k, col, taps):
        v = projected(k, col, block + HALO)
        total = taps[CONV - 1 : CONV] * v
        for j in range(1, CONV):
            total = total + same[j - 1, pl.ds(k * block, block + HALO), :] * (
                taps[CONV - 1 - j : CONV - j] * pltpu.roll(v, j, 0)
            )
        total = total[HALO:]
        return (total / (1.0 + jnp.exp(-total))).astype(bf)

    next_tile(1)

    partial(0).wait_recv()
    for k in range(4):
        for t in range(state // 128):
            at = pl.ds(pl.multiple_of(at_x * state + t * 128, 128), 128)
            bc[core, pl.ds(k * block, block), t * 128 : (t + 1) * 128] = convolved(
                k, t * 128, jnp.where(core == 0, tapbc_ref[:, 0, at], tapbc_ref[:, 1, at])
            )
    bc_copy = remote(bc.at[core], bc.at[core], bc_send, bc_recv, sibling)
    bc_copy.start()

    step_copy.wait_recv()
    heads = head_ref[2 * at_x + core]
    bias_col, decay_col = heads[0, :, 0:1], heads[1, :, 0:1]
    u = dt_own[...] + dt_got[...] + bias_col
    step_dt = jnp.maximum(u, 0.0) + jnp.log1p(jnp.exp(-jnp.abs(u)))
    rate = -step_dt * decay_col
    dt_t[...] = step_dt
    upper = jnp.where(
        lax.broadcasted_iota(jnp.int32, (block, block), 0)
        <= lax.broadcasted_iota(jnp.int32, (block, block), 1), 1.0, 0.0
    ).astype(bf)
    before = earlier[:, rows - 1 :]
    first_before = before
    passed = jnp.zeros((8, 1), f32)
    for k in range(4):
        here = slice(k * block, (k + 1) * block)
        r = rate[:, here]
        high = r.astype(bf)
        middle = (r - high.astype(f32)).astype(bf)
        low = (r - high.astype(f32) - middle.astype(f32)).astype(bf)
        three = jnp.dot(
            jnp.concatenate([high.astype(f32), middle.astype(f32), low.astype(f32)], axis=0).astype(bf),
            upper, preferred_element_type=f32,
        )
        cum = three[0:8] + three[8:16] + three[16:24]
        cum_t[:, here] = cum
        last = cum[:, block - 1 :]
        seg = seg_row(k)
        seg_last = seg[:, block - 1 :]
        at_last = jnp.where(seg == seg_last, 1.0, 0.0)
        w_t[:, here] = jnp.exp(last - cum) * step_dt[:, here] * at_last
        entry_t[:, here] = jnp.exp(cum) * jnp.where(seg == before, 1.0, 0.0)
        enter_t[:, here] = jnp.exp(cum + passed) * jnp.where(seg == first_before, 1.0, 0.0)
        keeps = jnp.where(seg_last == before, 1.0, 0.0)
        gain_t[k] = jnp.broadcast_to(jnp.exp(last) * keeps, (8, 128))
        passed = passed + last
        before = seg_last

    next_tile(2)
    bc_copy.wait_recv()
    bt[...] = bc[0].astype(f32).T.astype(bf)
    for k in range(4):
        here = pl.ds(k * block, block)
        scores[k] = jnp.dot(bc[1, here, :], bt[:, here], preferred_element_type=f32)

    lane = lax.broadcasted_iota(jnp.int32, (1, 128), 1)

    def pair_rows(ref, p, here):
        return ref[2 * p : 2 * p + 1, here], ref[2 * p + 1 : 2 * p + 2, here]

    def pair_column(ref, p, here):
        a, b = pair_rows(ref, p, here)
        return jnp.concatenate(
            [jnp.broadcast_to(a, (64, a.shape[1])), jnp.broadcast_to(b, (64, b.shape[1]))], axis=0
        ).T

    def state_copy(p):
        return remote(leaving.at[p], arriving.at[p], st_send.at[p], st_recv.at[p], y_dev[0])

    def scan_states(p):
        cols = slice(p * 128, (p + 1) * 128)
        at = aligned(at_x * group + core * share + p * 128, 128)
        taps = tapx_ref[:, at]
        now = jnp.zeros((state, 128), f32)
        for k in range(4):
            here = slice(k * block, (k + 1) * block)
            x = convolved(k, state + p * 128, taps)
            xs[here, cols] = x
            weighted = (pair_column(w_t, p, here) * x.astype(f32)).astype(bf)
            entering[k] = now.astype(bf)
            gain = jnp.where(lane < 64, gain_t[k, 2 * p : 2 * p + 1, :], gain_t[k, 2 * p + 1 : 2 * p + 2, :])
            now = gain * now + jnp.dot(bt[:, here], weighted, preferred_element_type=f32)
        leaving[p] = now.astype(bf)

        @pl.when(at_y == 0)
        def _():
            state_copy(p).start()

    def scan_blocks(p):
        cols = slice(p * 128, (p + 1) * 128)
        at_head = at_x * (group // HEAD_DIM) + core * (share // HEAD_DIM) + 2 * p
        skips = jnp.where(lane < 64, skip_ref[at_head], skip_ref[at_head + 1])
        for k in range(4):
            here = slice(k * block, (k + 1) * block)
            cum_rows, dt_rows = pair_rows(cum_t, p, here), pair_rows(dt_t, p, here)
            cum_cols = [column(r) for r in cum_rows]
            far = pair_column(entry_t, p, here) * jnp.dot(
                bc[1, here, :], entering[k], preferred_element_type=f32
            )
            for i in range(2):
                top = i * 128
                w = top + 128
                tall = slice(top, w)
                outs = []
                for n in range(2):
                    spans = jnp.concatenate([cum_cols[n][tall]] * (w // 128), axis=1)
                    spans = spans - cum_rows[n][:, :w] + bias[k, tall, :w]
                    mixing = (scores[k, tall, :w] * jnp.exp(spans) * dt_rows[n][:, :w]).astype(bf)
                    outs.append(
                        jnp.dot(mixing, xs[k * block : k * block + w, cols], preferred_element_type=f32)
                    )
                there = slice(k * block + top, k * block + w)
                ssd[there, cols] = (
                    jnp.where(lane < 64, outs[0], outs[1]) + far[tall]
                    + skips * xs[there, cols].astype(f32)
                )

    partial(1).wait_recv()
    scan_states(0)
    scan_blocks(0)
    scan_states(1)
    scan_blocks(1)
    next_tile(3)
    partial(2).wait_recv()
    scan_states(2)
    scan_blocks(2)
    scan_states(3)
    scan_blocks(3)
    next_tile(4)

    @pl.when(at_y == 1)
    def _():
        for p in range(4):
            state_copy(p).wait_recv()

    @pl.when(at_y == 0)
    def _():
        arriving[...] = jnp.zeros_like(arriving)

    at_panel = at_x * group + core * share

    def spread(j, k, to):
        return remote(
            gated_out.at[pl.ds(k * block, block), pl.ds(j * state, state)],
            whole.at[:, aligned(at_panel + j * state, state)],
            g_send.at[j, k], g_recv.at[j, 2 * at_x + core], to,
        )

    def arrives(j, src_x, src_c):
        return remote(
            gated_out.at[pl.ds(0, block), pl.ds(0, state)],
            whole.at[:, aligned(src_x * group + src_c * share + j * state, state)],
            g_send.at[j, 0], g_recv.at[j, 2 * src_x + src_c], sibling,
        )

    def sums_to(k, to):
        return remote(
            sum_sent.at[k], sums.at[2 * at_x + core], n_send.at[k], n_recv.at[2 * at_x + core], to
        )

    where = 2 * at_x + core

    def gate(j):
        for k in range(4):
            here = slice(k * block, (k + 1) * block)
            total = jnp.zeros((block, 128), f32) if j == 0 else square[here, :]
            for i in range(2):
                p = 2 * j + i
                cols = slice(p * 128, (p + 1) * 128)
                z = projected_z(k, j, i)
                held = pair_column(enter_t, p, here) * jnp.dot(
                    bc[1, here, :], arriving[p], preferred_element_type=f32
                )
                gated = (ssd[here, cols] + held) * (z / (1.0 + jnp.exp(-z)))
                total = total + gated * gated
                gated_out[here, cols] = (gated * chan_ref[0:1, aligned(at_panel + p * 128, 128)]).astype(bf)
            square[here, :] = total
            if j == 1:
                sum_sent[k] = jnp.broadcast_to(jnp.sum(total.T, axis=0, keepdims=True), (8, block))

            @pl.when(where != k)
            def _():
                spread(j, k, 4 * at_y + k).start()
                if j == 1:
                    sums_to(k, 4 * at_y + k).start()

            @pl.when(where == k)
            def _():
                whole[:, aligned(at_panel + j * state, state)] = gated_out[here, j * state : (j + 1) * state]
                if j == 1:
                    sums[k] = sum_sent[k]

    def projected_z(k, j, i):
        at = pl.ds(k * block + HALO, block)
        t = 3 + j
        total = own[at, pl.ds(t * state + i * 128, 128)] + got[t, at, pl.ds(i * 128, 128)].astype(f32)
        return total.astype(bf).astype(f32)

    partial(3).wait_recv()
    gate(0)
    partial(4).wait_recv()
    gate(1)

    for k in range(4):
        @pl.when(where != k)
        def _():
            for j in range(2):
                arrives(j, k // 2, k % 2).wait_recv()
            remote(
                sum_sent.at[k], sums.at[k], n_send.at[k], n_recv.at[k], sibling
            ).wait_recv()
            for j in range(2):
                spread(j, k, 4 * at_y + k).wait_send()
            sums_to(k, 4 * at_y + k).wait_send()

    for c in copies + [to_sibling, step_copy, bc_copy] + wsib + wstep:
        c.wait_send()
    for group_of in by_y + by_x + by_d + by_z + wfirst + wrest:
        for c in group_of:
            c.wait_send()
    for t in range(5):
        partial(t).wait_send()
    for slot in range(2):
        for f in range(CHUNKS):
            swap(slot, f).wait_send()

    @pl.when(at_y == 0)
    def _():
        for p in range(4):
            state_copy(p).wait_send()


def mix(tokens, source, segment, w_in, wdt, conv_x, conv_bc, heads, skip, chan):
    rows, depth = tokens.shape[0], w_in.shape[0]
    width = w_in.shape[1] // 5
    state = width // 4
    share = width // 2
    feats, kdim, span = 2 * depth, 4 * depth, 4 * rows
    ext = span + HALO
    f32, bf = jnp.float32, jnp.bfloat16
    vmem = pl.BlockSpec(memory_space=pltpu.VMEM)
    hbm = pl.BlockSpec(memory_space=pl.ANY)
    smem = pl.BlockSpec(memory_space=pltpu.SMEM)
    dma = pltpu.SemaphoreType.DMA

    def buf(shape, kind=f32):
        return pltpu.VMEM(shape, kind)

    return pl.pallas_call(
        mixer_kernel,
        out_shape=(
            jax.ShapeDtypeStruct((rows, 2 * width), bf),
            jax.ShapeDtypeStruct((4, 8, rows), f32),
        ),
        in_specs=[hbm, vmem, vmem, hbm, vmem, vmem, vmem, vmem, smem, vmem],
        out_specs=(vmem, vmem),
        scratch_shapes=[
            buf((8, rows), jnp.int32), buf((8, 8, rows), jnp.int32),
            buf((8 * rows, feats), bf), buf((8 * rows + HALO, 128), jnp.int32),
            buf((ext, 8 * rows), bf), buf((2, ext, kdim), bf),
            buf((kdim, 5 * state), bf), buf((16, kdim), bf), buf((kdim, 128), bf),
            buf((5, ext, state), bf), buf((5, ext, state), bf), buf((ext, 5 * state)),
            buf((8, span)), buf((8, span)), buf((8, span)),
            buf((3, ext, 128)), buf((2, span, state), bf), buf((state, span), bf),
            buf((span, share), bf), buf((4, rows, rows)), buf((4, rows, rows)),
            buf((8, span)), buf((8, span)), buf((8, span)), buf((8, span)), buf((8, span)),
            buf((4, 8, 128)), buf((4, state, 128), bf),
            buf((4, state, 128), bf), buf((4, state, 128), bf),
            buf((span, share)), buf((span, share), bf), buf((span, 128)), buf((4, 8, rows)),
            dma((2,)), dma((6,)), dma((7,)), dma((7,)),
            dma((2, CHUNKS)), dma((2, CHUNKS)), dma((2, CHUNKS)), dma((2, CHUNKS)),
            dma((2, CHUNKS)), dma((2, CHUNKS)), dma((4, CHUNKS)), dma((4, CHUNKS)),
            dma, dma, dma((3, 6)), dma((3, 6)), dma((2, 4)), dma((2, 4)), dma((5,)), dma((5,)), dma, dma,
            dma((2, CHUNKS)), dma((2, CHUNKS)), dma, dma, dma((4,)), dma((4,)),
            dma((2, 4)), dma((2, 4)), dma((4,)), dma((4,)),
        ],
        compiler_params=pltpu.CompilerParams(
            collective_id=0, has_side_effects=True, vmem_limit_bytes=60 << 20
        ),
    )(tokens, source, segment, w_in, wdt, conv_x, conv_bc, heads, skip, chan)


TILES = 4


def output_kernel(gated_ref, sums_ref, w_hbm, out_ref, wbuf, own, sent, got,
                  loc_sem, send_sem, recv_sem):
    m = lax.axis_index("mp")
    half = gated_ref.shape[0]
    chans = gated_ref.shape[1] // 2
    part = half // 4
    step = w_hbm.shape[0] // TILES

    barrier = pltpu.get_barrier_semaphore()
    for k in range(1, 4):
        pl.semaphore_signal(barrier, inc=1, device_id={"mp": (m + k) % 4}, device_id_type=MESH)
    loads = []
    for t in range(TILES):
        rows = pl.ds(t * step, step)
        loads.append(pltpu.make_async_copy(w_hbm.at[rows], wbuf.at[rows], loc_sem.at[t]))
        loads[t].start()
    scales = []
    for g in range(2):
        total = sums_ref[2 * g, 0:1, :] + sums_ref[2 * g + 1, 0:1, :]
        inv = column(lax.rsqrt(total * (1.0 / chans) + 1e-05))
        scales.append(jnp.concatenate([inv, inv], axis=1))
    pl.semaphore_wait(barrier, 3)

    inner = m * (3 - m) // 2
    end = inner * 3 * (m - 1) + (1 - inner) * m
    near = 1 + end // 3
    far = 3 - near
    opp = 3 - end

    def block(j):
        return pl.ds(pl.multiple_of(j * part, part), part)

    def hop(i, slot, to, t):
        c = pl.ds(t * step, step)
        return along_mp(
            sent.at[i, :, c], got.at[slot, :, c], send_sem.at[i, t], recv_sem.at[slot, t], to
        )

    for t in range(TILES):
        loads[t].wait()

        @pl.loop(0, step // 256)
        def _(u):
            c = pl.ds(pl.multiple_of(t * step + u * 256, 256), 256)
            sides = [
                lax.dot_general(
                    gated_ref[:, g * chans : (g + 1) * chans], wbuf[c, g * chans : (g + 1) * chans],
                    (((1,), (1,)), ((), ())), preferred_element_type=jnp.float32,
                )
                for g in range(2)
            ]
            own[:, c] = sides[0] * scales[0] + sides[1] * scales[1]

        c = pl.ds(t * step, step)

        @pl.when(inner == 0)
        def _():
            for slot, j in ((2, opp), (1, far), (0, near)):
                sent[slot, :, c] = own[block(j), c].astype(jnp.bfloat16)
                hop(slot, slot, near, t).start()

        @pl.when(inner == 1)
        def _():
            sent[0, :, c] = own[block(end), c].astype(jnp.bfloat16)
            hop(0, 0, end, t).start()

    @pl.when(inner == 1)
    def _():
        for t in range(TILES):
            c = pl.ds(t * step, step)
            for i, slot, j in ((1, 1, opp), (2, 3, far)):
                held = 2 if i == 1 else 1
                hop(i, held, j, t).wait_recv()
                sent[i, :, c] = (
                    own[block(j), c] + got[held, :, c].astype(jnp.float32)
                ).astype(jnp.bfloat16)
                hop(i, slot, j, t).start()
        for t in range(TILES):
            c = pl.ds(t * step, step)
            hop(0, 0, end, t).wait_recv()
            hop(0, 3, end, t).wait_recv()
            out_ref[:, c] = (
                own[block(m), c] + got[0, :, c].astype(jnp.float32)
                + got[3, :, c].astype(jnp.float32)
            ).astype(jnp.bfloat16)

    @pl.when(inner == 0)
    def _():
        for t in range(TILES):
            c = pl.ds(t * step, step)
            hop(0, 0, near, t).wait_recv()
            hop(0, 1, near, t).wait_recv()
            out_ref[:, c] = (
                own[block(m), c] + got[0, :, c].astype(jnp.float32)
                + got[1, :, c].astype(jnp.float32)
            ).astype(jnp.bfloat16)

    for t in range(TILES):
        for i in range(3):
            hop(i, 0, near * (1 - inner) + end * inner, t).wait_send()


def project_out(gated, sums, w_out):
    half, chans = gated.shape
    feats = w_out.shape[0]
    bf = jnp.bfloat16
    vmem = pl.BlockSpec(memory_space=pltpu.VMEM)
    dma = pltpu.SemaphoreType.DMA
    return pl.pallas_call(
        output_kernel,
        out_shape=jax.ShapeDtypeStruct((half // 4, feats), bf),
        in_specs=[vmem, vmem, pl.BlockSpec(memory_space=pl.ANY)],
        out_specs=vmem,
        scratch_shapes=[
            pltpu.VMEM((feats, chans), bf),
            pltpu.VMEM((half, feats), jnp.float32),
            pltpu.VMEM((3, half // 4, feats), bf),
            pltpu.VMEM((4, half // 4, feats), bf),
            dma((TILES,)), dma((3, TILES)), dma((4, TILES)),
        ],
        compiler_params=pltpu.CompilerParams(
            collective_id=1, has_side_effects=True, vmem_limit_bytes=48 << 20
        ),
    )(gated, sums, w_out)


def on_plane(
    tokens, pack_source, segment_ids, w_in, w_dt, w_out, conv_x, conv_bc,
    dt_bias, decay_rate, skip_gain, norm_gain,
):
    heads = w_dt.shape[1] // 4
    wdt = w_dt.T.reshape(4, heads, w_dt.shape[0])
    wdt = jnp.pad(wdt, ((0, 0), (0, 16 - heads), (0, 0)))
    params = jnp.stack([dt_bias, decay_rate]).reshape(2, 4, heads).transpose(1, 0, 2)
    params = jnp.broadcast_to(params[:, :, :, None], (4, 2, heads, 128))
    gated, sums = mix(
        tokens, pack_source.reshape(1, -1), segment_ids.reshape(1, -1), w_in, wdt,
        conv_x, conv_bc, params, skip_gain, norm_gain.reshape(1, -1),
    )
    return project_out(gated, sums, w_out)


def solution(mesh):
    placed = (
        P("dp", None),
        P("dp"),
        P("dp"),
        P("dp", "mp"),
        P("dp", "mp"),
        P(None, "mp"),
        P(None, "mp"),
        P(None, None, "mp"),
        P("mp"),
        P("mp"),
        P("mp"),
        P("mp"),
    )
    body = on_plane if mesh.shape["dp"] == 8 and mesh.shape["mp"] == 4 else on_device
    return jax.shard_map(
        body, mesh=mesh, in_specs=placed, out_specs=P(("dp", "mp"), None), check_vma=False
    )
```

```python
import jax
import jax.numpy as jnp
from jax import lax
from jax.experimental import pallas as pl
from jax.experimental.pallas import tpu as pltpu
from jax.sharding import PartitionSpec as P

HEAD_DIM = 64
STATE = 256
CONV = 4
BLOCK = 256


highest = lax.Precision.HIGHEST


def passed_along(x, axis, by):
    size = lax.axis_size(axis)
    pairs = [(i, i + by) for i in range(size) if 0 <= i + by < size]
    return lax.ppermute(x, axis, pairs)


def carried_in(x, axis, join, neutral):
    place = lax.axis_index(axis)
    gathered = jax.tree.map(
        lambda a, kind: lax.all_gather(a.astype(kind), axis), x, (jnp.bfloat16, jnp.bfloat16)
    )
    state = jax.tree.map(lambda a, e: jnp.zeros_like(a) + jnp.asarray(e, a.dtype), x, neutral)

    def one(hop, state):
        return join(
            state,
            jax.tree.map(
                lambda a, own: lax.dynamic_index_in_dim(a, hop, 0, False).astype(own.dtype),
                gathered,
                x,
            ),
        )

    return lax.fori_loop(0, place, one, state)


def chain_combine(earlier, later_part):
    return (earlier[0] * later_part[0], later_part[0][:, None, None] * earlier[1] + later_part[1])


def running_sum(values):
    places = jnp.arange(values.shape[0])
    lower = (places[:, None] >= places[None, :]).astype(values.dtype)
    return jnp.dot(lower, values, precision=highest)


def block_step(carry, pieces):
    state_now, prev_seg = carry
    x_block, b_block, c_block, step_dt, step_rate, seg_block = pieces
    per_group = x_block.shape[1] // b_block.shape[1]
    cum_rate = running_sum(step_rate)
    places = jnp.arange(seg_block.shape[0])
    linked = (seg_block[:, None] == seg_block[None, :]) & (places[:, None] >= places[None, :])
    log_spans = cum_rate.T[:, :, None] - cum_rate.T[:, None, :]
    decay_mat = jnp.where(linked[None], jnp.exp(jnp.where(linked[None], log_spans, 0.0)), 0.0)
    scores = jnp.einsum("tgn,sgn->gts", c_block, b_block, preferred_element_type=jnp.float32)
    scores = jnp.repeat(scores, per_group, axis=0)
    mixing = (scores * decay_mat * step_dt.T[:, None, :]).astype(jnp.bfloat16)
    in_block = jnp.einsum("hts,shp->thp", mixing, x_block, preferred_element_type=jnp.float32)
    c_heads = jnp.repeat(c_block.astype(jnp.float32), per_group, axis=1)
    b_heads = jnp.repeat(b_block.astype(jnp.float32), per_group, axis=1)
    entry_mask = jnp.where((seg_block == prev_seg)[:, None], jnp.exp(cum_rate), 0.0)
    from_before = entry_mask[:, :, None] * jnp.einsum(
        "thn,hpn->thp", c_heads, state_now, precision=highest
    )
    last_seg = seg_block[-1]
    weight = (
        jnp.where((seg_block == last_seg)[:, None], jnp.exp(cum_rate[-1][None, :] - cum_rate), 0.0)
        * step_dt
    )
    carried = jnp.where(last_seg == prev_seg, jnp.exp(cum_rate[-1]), 0.0)
    added_in = jnp.einsum(
        "shp,shn->hpn", weight[:, :, None] * x_block.astype(jnp.float32), b_heads, precision=highest
    )
    return ((carried[:, None, None] * state_now + added_in, last_seg), in_block + from_before)


def on_device(
    tokens,
    pack_source,
    segment_ids,
    w_in,
    w_dt,
    w_out,
    conv_x,
    conv_bc,
    dt_bias,
    decay_rate,
    skip_gain,
    norm_gain,
):
    row_count = tokens.shape[0]
    data_devs = lax.axis_size("dp")
    capacity = 2 * row_count // data_devs
    source_dev = pack_source // row_count
    source_row = pack_source % row_count
    same_source = source_dev[:, None] == source_dev[None, :]
    earlier_rows = pack_source[None, :] < pack_source[:, None]
    rank_in = jnp.sum((same_source & earlier_rows).astype(jnp.int32), axis=1)
    slot_index = source_dev * capacity + rank_in
    requests = (
        jnp.full((data_devs * capacity,), -1, jnp.int32)
        .at[slot_index]
        .set(source_row)
        .reshape(data_devs, capacity)
    )
    wanted = lax.all_to_all(requests, "dp", split_axis=0, concat_axis=0, tiled=True)
    fetched = jnp.where(
        (wanted >= 0)[:, :, None], tokens[jnp.maximum(wanted, 0)], jnp.zeros((), jnp.bfloat16)
    )
    replies = lax.all_to_all(fetched, "dp", split_axis=0, concat_axis=0, tiled=True)
    gathered = replies.reshape(data_devs * capacity, tokens.shape[1])[slot_index]
    panel_cols = w_in.shape[1]
    head_count = w_dt.shape[1]
    chan_width = w_out.shape[1]
    proj_sum = jnp.dot(
        gathered, lax.all_gather(w_in, "dp", axis=0, tiled=True), preferred_element_type=jnp.float32
    )
    step_sum = jnp.dot(
        gathered, lax.all_gather(w_dt, "dp", axis=0, tiled=True), preferred_element_type=jnp.float32
    )
    proj_sum, dt_raw = (proj_sum, step_sum)
    projected = proj_sum.astype(jnp.bfloat16)
    group_width = (panel_cols - 2 * chan_width) // 2
    gate_in = projected[:, chan_width : 2 * chan_width]
    stacked = jnp.concatenate([projected[:, :chan_width], projected[:, 2 * chan_width :]], axis=1)
    tail_len = CONV - 1
    tail_vals = stacked[row_count - tail_len :].astype(jnp.float32)
    tail_seg = (segment_ids[row_count - tail_len :] + 1).astype(jnp.float32)
    prev_vals, prev_seg = passed_along((tail_vals, tail_seg), "dp", 1)
    extended = jnp.concatenate([prev_vals.astype(jnp.bfloat16), stacked], axis=0)
    seg_ext = jnp.concatenate([prev_seg.astype(jnp.int32) - 1, segment_ids], axis=0)
    kernel = jnp.concatenate([conv_x, conv_bc.reshape(CONV, 2 * group_width)], axis=1)
    conv_sum = jnp.zeros((row_count, stacked.shape[1]), jnp.float32)
    for lag_index in range(CONV):
        same_seg = (seg_ext[lag_index : lag_index + row_count] == segment_ids)[:, None]
        conv_sum = conv_sum + jnp.where(
            same_seg,
            kernel[lag_index][None, :]
            * extended[lag_index : lag_index + row_count].astype(jnp.float32),
            0.0,
        )
    convolved = jax.nn.silu(conv_sum).astype(jnp.bfloat16)
    local_groups = group_width // STATE
    x_all = convolved[:, :chan_width].reshape(row_count, head_count, HEAD_DIM)
    b_all = convolved[:, chan_width : chan_width + group_width].reshape(
        row_count, local_groups, STATE
    )
    c_all = convolved[:, chan_width + group_width :].reshape(row_count, local_groups, STATE)
    step_dt = jax.nn.softplus(dt_raw + dt_bias)
    step_rate = -step_dt * decay_rate
    seg_before = seg_ext[tail_len - 1]
    block_total = row_count // BLOCK

    def to_blocks(values):
        return values.reshape((block_total, BLOCK) + values.shape[1:])

    start_state = (jnp.zeros((head_count, HEAD_DIM, STATE), jnp.float32), seg_before)
    final, outputs = lax.scan(
        block_step,
        start_state,
        (
            to_blocks(x_all),
            to_blocks(b_all),
            to_blocks(c_all),
            to_blocks(step_dt),
            to_blocks(step_rate),
            to_blocks(segment_ids),
        ),
    )
    local_state = final[0]
    scan_out = outputs.reshape(row_count, head_count, HEAD_DIM)
    running = running_sum(step_rate)
    carry_gain = jnp.where(segment_ids[-1] == seg_before, jnp.exp(running[-1]), 0.0)
    neutral = (jnp.ones((head_count,), jnp.float32), jnp.zeros_like(local_state))
    incoming = carried_in((carry_gain, local_state), "dp", chain_combine, neutral)[1]
    c_heads = jnp.repeat(c_all.astype(jnp.float32), head_count // local_groups, axis=1)
    entry_mask = jnp.where((segment_ids == seg_before)[:, None], jnp.exp(running), 0.0)
    scan_out = scan_out + entry_mask[:, :, None] * jnp.einsum(
        "thn,hpn->thp", c_heads, incoming, precision=highest
    )
    scan_out = scan_out + skip_gain[None, :, None] * x_all.astype(jnp.float32)
    gated_out = scan_out.reshape(row_count, chan_width) * jax.nn.silu(gate_in.astype(jnp.float32))
    grouped = gated_out.reshape(row_count, local_groups, chan_width // local_groups)
    inv_rms = lax.rsqrt(jnp.mean(grouped * grouped, axis=2, keepdims=True) + 1e-05)
    normed = ((grouped * inv_rms).reshape(row_count, chan_width) * norm_gain).astype(jnp.bfloat16)
    return lax.psum_scatter(
        lax.dot_general(
            normed, w_out, (((1,), (1,)), ((), ())), preferred_element_type=jnp.float32
        ).astype(jnp.bfloat16),
        "mp",
        scatter_dimension=0,
        tiled=True,
    )


HALO = 16
CHUNKS = 4
MESH = pl.DeviceIdType.MESH


def remote(src, dst, send, recv, dp):
    return pltpu.make_async_remote_copy(
        src_ref=src, dst_ref=dst, send_sem=send, recv_sem=recv,
        device_id={"dp": dp}, device_id_type=MESH,
    )


def along_mp(src, dst, send, recv, mp):
    return pltpu.make_async_remote_copy(
        src_ref=src, dst_ref=dst, send_sem=send, recv_sem=recv,
        device_id={"mp": mp}, device_id_type=MESH,
    )


def column(row):
    return jnp.broadcast_to(row, (128, row.shape[1])).T


def aligned(start, size):
    return pl.ds(pl.multiple_of(start, 128), size)


TILES = 4
HOPS = 2 * TILES


def mixer_kernel(
    tok_hbm, source_ref, segment_ref, w_hbm, wdt_ref, tapx_ref, tapbc_ref, dtb_ref, decay_ref, skip_ref,
    chan_ref, wout_hbm,
    out_ref,
    meta_ref, metas, tokg, idxcol, onehot, packed, wbuf, wdt_all, wdtt, wdtc, sent, got, own,
    dt_sent, dt_got, dt_own, same, bc, bt, xs, scores, bias, head_cols,
    cum_t, dt_t, w_t, entry_t, enter_t, gain_t, entering, leaving, arriving, ssd, gated_out, square, sum_sent,
    whole, sums, out_sent, out_got,
    loc_sem, wloc_sem, meta_send, meta_recv, y_send, y_recv, x_send, x_recv, d_send, d_recv, z_send, z_recv,
    s_send, s_recv, w_send, w_recv, v_send, v_recv, p_send, p_recv, t_send, t_recv, q_send, q_recv,
    bc_send, bc_recv, st_send, st_recv, g_send, g_recv, n_send, n_recv, out_sem, o_send, o_recv,
):
    f32, bf = jnp.float32, jnp.bfloat16
    me, m = lax.axis_index("dp"), lax.axis_index("mp")
    core = me % 2
    at_x = (me // 2) % 2
    at_y = me // 4
    sibling = me + 1 - 2 * core
    beside = m + 1 - 2 * (m % 2)
    half = m % 2
    x_dev = [4 * at_y + 2 * (1 - at_x) + c for c in (core, 1 - core)]
    y_dev = [4 * (1 - at_y) + 2 * at_x + c for c in (core, 1 - core)]
    d_dev = [4 * (1 - at_y) + 2 * (1 - at_x) + c for c in (core, 1 - core)]
    cores = (core, 1 - core)

    rows, depth = tok_hbm.shape[0], w_hbm.shape[0]
    width = w_hbm.shape[1] // 5
    group, state = width, width // 4
    share = group // 2
    feats = 2 * depth
    kdim = 2 * feats
    span = 4 * rows
    ext = span + HALO
    part = rows // 2
    chunk = feats // CHUNKS
    block = rows

    barrier = pltpu.get_barrier_semaphore()
    for k in range(1, 8):
        pl.semaphore_signal(barrier, inc=1, device_id={"dp": (me + k) % 8}, device_id_type=MESH)
    for k in range(1, 4):
        pl.semaphore_signal(barrier, inc=1, device_id={"mp": (m + k) % 4}, device_id_type=MESH)
    meta_ref[...] = jnp.concatenate(
        [source_ref[...], segment_ref[...], jnp.zeros((6, rows), jnp.int32)], axis=0
    )

    pieces = (
        (0, 128), (128, 128), (state, state), (2 * state, state), (3 * state, state),
        (4 * state, 128), (4 * state + 128, 128),
    )
    regions = ((0, state), (state, share), (state + share, share))
    final = len(pieces) - 1

    def of_columns(x, c, col):
        if col < state:
            return 4 * width + c * 2 * state + x * state + col
        if col < state + share:
            return x * group + c * share + col - state
        return 2 * width + x * group + c * share + col - state - share

    for g in range(4):
        wdt_all[g] = jnp.concatenate(
            [wdt_ref[8 * g : 8 * g + 8, :].astype(f32), jnp.zeros((8, depth), f32)], axis=0
        ).astype(bf)
    head_cols[0] = column(dtb_ref[...])
    head_cols[1] = column(decay_ref[...])

    kmine = pl.ds(pl.multiple_of(depth * (2 * at_x + core), depth), depth)
    wlocal = [
        pltpu.make_async_copy(
            w_hbm.at[:, aligned(of_columns(at_x, core, col), size)],
            wbuf.at[kmine, pl.ds(col, size)], wloc_sem.at[i],
        )
        for i, (col, size) in enumerate(regions)
    ]
    wlocal.append(pltpu.make_async_copy(wdt_all.at[2 * at_x + core], wdtt.at[:, kmine], wloc_sem.at[3]))
    mine_rows = pl.ds(pl.multiple_of(me * rows, rows), rows)

    def features(y, c, f, size):
        return aligned(y * kdim + c * feats + f * chunk, size)

    local_tok = pltpu.make_async_copy(
        tok_hbm.at[:, features(at_y, core, 0, feats)], tokg.at[mine_rows], loc_sem.at[0]
    )
    local_tok.start()
    for c in wlocal:
        c.start()
    pl.semaphore_wait(barrier, 10)

    copies = []
    for k in range(1, 8):
        copies.append(
            remote(meta_ref, metas.at[me], meta_send.at[k - 1], meta_recv.at[k - 1], (me + k) % 8)
        )
    local_meta = pltpu.make_async_copy(meta_ref, metas.at[me], loc_sem.at[1])
    for c in copies + [local_meta]:
        c.start()

    def half_rows(dev, which):
        return pl.ds(pl.multiple_of(dev * rows + which * part, part), part)

    def fcols(f):
        return pl.ds(f * chunk, chunk)

    by_y, by_x, by_d, by_z = [[], []], [], [], []
    for f in range(CHUNKS):
        for side, passing in enumerate((half, 1 - half)):
            by_y[side].append([
                remote(
                    tok_hbm.at[pl.ds(pl.multiple_of(passing * part, part), part),
                               features(1 - at_y, cores[r], f, chunk)],
                    tokg.at[half_rows(me, passing), fcols(f)],
                    y_send.at[2 * side + r, f], y_recv.at[2 * side + r, f], y_dev[r],
                )
                for r in range(2)
            ])
        by_x.append([
            remote(
                tok_hbm.at[pl.ds(pl.multiple_of(half * part, part), part),
                           features(at_y, cores[r], f, chunk)],
                tokg.at[half_rows(me, half), fcols(f)],
                x_send.at[r, f], x_recv.at[r, f], x_dev[r],
            )
            for r in range(2)
        ])
        by_d.append([
            remote(
                tokg.at[half_rows(y_dev[r], half), fcols(f)], tokg.at[half_rows(y_dev[r], half), fcols(f)],
                d_send.at[r, f], d_recv.at[r, f], x_dev[0],
            )
            for r in range(2)
        ])
        by_z.append([
            along_mp(
                tokg.at[half_rows(dev, half), fcols(f)], tokg.at[half_rows(dev, half), fcols(f)],
                z_send.at[i, f], z_recv.at[i, f], beside,
            )
            for i, dev in enumerate(x_dev + d_dev)
        ])
    def begin(group_of):
        for c in group_of:
            c.start()

    begin(by_y[0][0] + by_x[0] + by_y[0][1] + by_x[1] + by_y[0][2] + by_y[0][3])
    for f in range(CHUNKS):
        begin(by_y[1][f])
    to_sibling = remote(
        tok_hbm.at[:, features(at_y, 1 - core, 0, feats)], tokg.at[mine_rows],
        s_send, s_recv, sibling,
    )
    to_sibling.start()
    wsib = [
        remote(
            w_hbm.at[:, aligned(of_columns(at_x, 1 - core, col), size)],
            wbuf.at[kmine, pl.ds(col, size)], w_send.at[0, i], w_recv.at[0, i], sibling,
        )
        for i, (col, size) in enumerate(regions)
    ]
    wsib.append(
        remote(wdt_all.at[2 * at_x + 1 - core], wdtt.at[:, kmine], w_send.at[0, 3], w_recv.at[0, 3], sibling)
    )
    for c in wsib:
        c.start()

    quarter = depth // 4
    wfirst = [
        [
            remote(
                w_hbm.at[pl.ds(q * quarter, quarter), aligned(of_columns(1 - at_x, cores[r], 0), 128)],
                wbuf.at[pl.ds(pl.multiple_of(depth * (2 * at_x + core) + q * quarter, quarter), quarter),
                        pl.ds(0, 128)],
                v_send.at[r, q], v_recv.at[r, q], x_dev[r],
            )
            for r in range(2)
        ]
        for q in range(4)
    ]
    wrest = [
        [
            remote(
                w_hbm.at[:, aligned(of_columns(1 - at_x, cores[r], col), size)],
                wbuf.at[kmine, pl.ds(col, size)],
                w_send.at[1 + r, i], w_recv.at[1 + r, i], x_dev[r],
            )
            for r in range(2)
        ]
        for i, (col, size) in enumerate(pieces) if i > 0
    ]
    wstep = [
        remote(
            wdt_all.at[2 * (1 - at_x) + cores[r]], wdtt.at[:, kmine],
            w_send.at[1 + r, 0], w_recv.at[1 + r, 0], x_dev[r],
        )
        for r in range(2)
    ]

    def index_column():
        for c in copies:
            c.wait_recv()
        local_meta.wait()
        idxcol[0:HALO, :] = jnp.full((HALO, 128), -1, jnp.int32)
        for j in range(8):
            idxcol[HALO + j * rows : HALO + (j + 1) * rows, :] = column(metas[j, 0:1, :])

    lane_row = lax.broadcasted_iota(jnp.int32, (1, 128), 1)

    def choose(which, quarter):
        steps = 8 * rows // 128 // 4

        @pl.loop(quarter * steps, (quarter + 1) * steps)
        def _(t):
            ids = idxcol[pl.ds(pl.multiple_of(which * span, span), ext), :]
            onehot[:, pl.ds(pl.multiple_of(t * 128, 128), 128)] = jnp.where(
                ids == lane_row + t * 128, 1.0, 0.0
            ).astype(bf)

    def place(f):
        return pl.ds(pl.multiple_of(core * feats + f * chunk, 128), chunk)

    def swap(slot, f):
        there = packed.at[slot, :, place(f)]
        return remote(there, there, q_send.at[slot, f], q_recv.at[slot, f], sibling)

    def pack(slot, f):
        packed[slot, :, place(f)] = jnp.dot(
            onehot[...], tokg[:, fcols(f)], preferred_element_type=f32
        ).astype(bf)
        swap(slot, f).start()


    def y_stage(f):
        for r in range(2):
            by_y[0][f][r].wait_recv()
            by_d[f][r].start()

    def x_stage(f):
        for r in range(2):
            by_x[f][r].wait_recv()
            by_z[f][r].start()

    def d_stage(f):
        for r in range(2):
            by_d[f][r].wait_recv()
            by_z[f][2 + r].start()

    def last_stage(f):
        for c in by_y[1][f] + by_z[f]:
            c.wait_recv()
        pack(0, f)

    x_stage(0)
    y_stage(0)
    begin(by_x[2])
    index_column()
    x_stage(1)
    y_stage(1)
    choose(1 - at_y, 0)
    d_stage(0)
    y_stage(2)
    begin(by_x[3])
    choose(1 - at_y, 1)
    x_stage(2)
    y_stage(3)
    for group_of in wfirst + [wstep] + wrest:
        begin(group_of)
    choose(1 - at_y, 2)
    d_stage(1)
    choose(1 - at_y, 3)
    local_tok.wait()
    to_sibling.wait_recv()
    last_stage(0)
    d_stage(2)
    last_stage(1)
    x_stage(3)
    last_stage(2)
    d_stage(3)
    last_stage(3)

    order = (2 * (1 - at_x), 2 * (1 - at_x) + 1, 2 * at_x + 1 - core, 2 * at_x + core)

    def block_rows(k):
        return pl.ds(pl.multiple_of(k * block, block), block)

    def block_ext(k):
        return pl.ds(pl.multiple_of(k * block + HALO, HALO), block)

    def product(slot, i):
        col, size = pieces[i]
        return jnp.dot(packed[slot], wbuf[:, pl.ds(col, size)], preferred_element_type=f32)

    def partial(i):
        col, size = pieces[i]
        if i < final:
            at = pl.ds(0, ext) if i < 4 else pl.ds(HALO, span)
            spots = [(at, i)]
        else:
            spots = [(block_ext(k), final + n) for n, k in enumerate(order)]
        return [
            remote(
                sent.at[at, pl.ds(col, size)], got.at[at, pl.ds(col, size)],
                p_send.at[n], p_recv.at[n], y_dev[0],
            )
            for at, n in spots
        ]

    partials = [partial(i) for i in range(len(pieces))]

    def theirs(i):
        if i > 0:
            for c in wrest[i - 1]:
                c.wait_recv()
        sent[:, pl.ds(*pieces[i])] = product(0, i).astype(bf)
        for c in partials[i]:
            c.start()

    def ours(i):
        own[:, pl.ds(*pieces[i])] = product(1, i)

    step_copy = remote(dt_sent, dt_got, t_send, t_recv, y_dev[0])

    for c in wlocal:
        c.wait()
    for c in wsib:
        c.wait_recv()
    for q in range(4):
        for c in wfirst[q]:
            c.wait_recv()
    for f in range(CHUNKS):
        swap(0, f).wait_recv()
    theirs(0)
    for c in wstep:
        c.wait_recv()
    wdtc[...] = jnp.concatenate(
        [wdtt[...].astype(f32), jnp.zeros((112, kdim), f32)], axis=0
    ).T.astype(bf)
    dt_sent[...] = jnp.dot(packed[0, HALO:, :], wdtc[...], preferred_element_type=f32).T[0:8]
    step_copy.start()
    theirs(1)

    for q in range(4):
        choose(at_y, q)
    for f in range(CHUNKS):
        pack(1, f)

    theirs(2)
    for f in range(CHUNKS):
        swap(1, f).wait_recv()
    ours(0)
    ours(1)
    dt_own[...] = jnp.dot(packed[1, HALO:, :], wdtc[...], preferred_element_type=f32).T[0:8]

    def seg_row(k):
        return metas[4 * at_y + k, 1:2, :]

    earlier = metas[(4 * at_y + 7) % 8, 1:2, :] * at_y - (1 - at_y)
    seg_ext = jnp.concatenate(
        [column(earlier)[rows - HALO :]] + [column(seg_row(k)) for k in range(4)], axis=0
    )
    for k in range(1, CONV):
        same[k - 1] = jnp.where(pltpu.roll(seg_ext, k, 0) == seg_ext, 1.0, 0.0)
    for k in range(4):
        seg_col = column(seg_row(k))
        for t in range(2):
            here = slice(t * 128, (t + 1) * 128)
            linked = (seg_col == seg_row(k)[:, here]) & (
                lax.broadcasted_iota(jnp.int32, (block, 128), 0)
                >= lax.broadcasted_iota(jnp.int32, (block, 128), 1) + t * 128
            )
            bias[k, :, here] = jnp.where(linked, 0.0, -1e30)

    def arrived(i):
        for c in partials[i]:
            c.wait_recv()

    def projected(k, col, size):
        at = pl.ds(k * block, size)
        cols = pl.ds(col, 128)
        return (own[at, cols] + got[at, cols].astype(f32)).astype(bf).astype(f32)

    def convolved(k, col, taps):
        v = projected(k, col, block + HALO)
        total = taps[CONV - 1 : CONV] * v
        for j in range(1, CONV):
            total = total + same[j - 1, pl.ds(k * block, block + HALO), :] * (
                taps[CONV - 1 - j : CONV - j] * pltpu.roll(v, j, 0)
            )
        total = total[HALO:]
        return (total / (1.0 + jnp.exp(-total))).astype(bf)

    arrived(0)
    arrived(1)
    for k in range(4):
        for t in range(state // 128):
            at = pl.ds(pl.multiple_of(at_x * state + t * 128, 128), 128)
            bc[core, pl.ds(k * block, block), t * 128 : (t + 1) * 128] = convolved(
                k, t * 128, jnp.where(core == 0, tapbc_ref[:, 0, at], tapbc_ref[:, 1, at])
            )
    bc_copy = remote(bc.at[core], bc.at[core], bc_send, bc_recv, sibling)
    bc_copy.start()

    step_copy.wait_recv()
    my_heads = pl.ds(pl.multiple_of(8 * (2 * at_x + core), 8), 8)
    bias_col, decay_col = head_cols[0, my_heads, :][:, 0:1], head_cols[1, my_heads, :][:, 0:1]
    u = dt_own[...] + dt_got[...] + bias_col
    step_dt = jnp.maximum(u, 0.0) + jnp.log1p(jnp.exp(-jnp.abs(u)))
    rate = -step_dt * decay_col
    dt_t[...] = step_dt
    upper = jnp.where(
        lax.broadcasted_iota(jnp.int32, (block, block), 0)
        <= lax.broadcasted_iota(jnp.int32, (block, block), 1), 1.0, 0.0
    ).astype(bf)
    before = earlier[:, rows - 1 :]
    first_before = before
    passed = jnp.zeros((8, 1), f32)
    for k in range(4):
        here = slice(k * block, (k + 1) * block)
        r = rate[:, here]
        high = r.astype(bf)
        middle = (r - high.astype(f32)).astype(bf)
        low = (r - high.astype(f32) - middle.astype(f32)).astype(bf)
        three = jnp.dot(
            jnp.concatenate([high.astype(f32), middle.astype(f32), low.astype(f32)], axis=0).astype(bf),
            upper, preferred_element_type=f32,
        )
        cum = three[0:8] + three[8:16] + three[16:24]
        cum_t[:, here] = cum
        last = cum[:, block - 1 :]
        seg = seg_row(k)
        seg_last = seg[:, block - 1 :]
        at_last = jnp.where(seg == seg_last, 1.0, 0.0)
        w_t[:, here] = jnp.exp(last - cum) * step_dt[:, here] * at_last
        entry_t[:, here] = jnp.exp(cum) * jnp.where(seg == before, 1.0, 0.0)
        enter_t[:, here] = jnp.exp(cum + passed) * jnp.where(seg == first_before, 1.0, 0.0)
        keeps = jnp.where(seg_last == before, 1.0, 0.0)
        gain_t[k] = jnp.broadcast_to(jnp.exp(last) * keeps, (8, 128))
        passed = passed + last
        before = seg_last

    theirs(3)
    ours(2)
    bc_copy.wait_recv()
    bt[...] = bc[0].astype(f32).T.astype(bf)
    for k in range(4):
        here = pl.ds(k * block, block)
        scores[k] = jnp.dot(bc[1, here, :], bt[:, here], preferred_element_type=f32)

    lane = lax.broadcasted_iota(jnp.int32, (1, 128), 1)

    def pair_rows(ref, p, here):
        return ref[2 * p : 2 * p + 1, here], ref[2 * p + 1 : 2 * p + 2, here]

    def pair_column(ref, p, here):
        a, b = pair_rows(ref, p, here)
        return jnp.concatenate(
            [jnp.broadcast_to(a, (64, a.shape[1])), jnp.broadcast_to(b, (64, b.shape[1]))], axis=0
        ).T

    def state_copy(p):
        return remote(leaving.at[p], arriving.at[p], st_send.at[p], st_recv.at[p], y_dev[0])

    def scan_states(p):
        cols = slice(p * 128, (p + 1) * 128)
        at = aligned(at_x * group + core * share + p * 128, 128)
        taps = tapx_ref[:, at]
        now = jnp.zeros((state, 128), f32)
        for k in range(4):
            here = slice(k * block, (k + 1) * block)
            x = convolved(k, state + p * 128, taps)
            xs[here, cols] = x
            weighted = (pair_column(w_t, p, here) * x.astype(f32)).astype(bf)
            entering[p % 2, k] = now.astype(bf)
            gain = jnp.where(lane < 64, gain_t[k, 2 * p : 2 * p + 1, :], gain_t[k, 2 * p + 1 : 2 * p + 2, :])
            now = gain * now + jnp.dot(bt[:, here], weighted, preferred_element_type=f32)
        leaving[p] = now.astype(bf)

        @pl.when(at_y == 0)
        def _():
            state_copy(p).start()

    def scan_blocks(p):
        cols = slice(p * 128, (p + 1) * 128)
        at_head = at_x * (group // HEAD_DIM) + core * (share // HEAD_DIM) + 2 * p
        skips = jnp.where(lane < 64, skip_ref[at_head], skip_ref[at_head + 1])
        for k in range(4):
            here = slice(k * block, (k + 1) * block)
            cum_rows, dt_rows = pair_rows(cum_t, p, here), pair_rows(dt_t, p, here)
            cum_cols = [column(r) for r in cum_rows]
            far = pair_column(entry_t, p, here) * jnp.dot(
                bc[1, here, :], entering[p % 2, k], preferred_element_type=f32
            )
            for i in range(2):
                top = i * 128
                w = top + 128
                tall = slice(top, w)
                outs = []
                for n in range(2):
                    spans = jnp.concatenate([cum_cols[n][tall]] * (w // 128), axis=1)
                    spans = spans - cum_rows[n][:, :w] + bias[k, tall, :w]
                    mixing = (scores[k, tall, :w] * jnp.exp(spans) * dt_rows[n][:, :w]).astype(bf)
                    outs.append(
                        jnp.dot(mixing, xs[k * block : k * block + w, cols], preferred_element_type=f32)
                    )
                there = slice(k * block + top, k * block + w)
                ssd[there, cols] = (
                    jnp.where(lane < 64, outs[0], outs[1]) + far[tall]
                    + skips * xs[there, cols].astype(f32)
                )

    arrived(2)
    scan_states(0)
    scan_states(1)
    scan_blocks(0)
    theirs(4)
    scan_blocks(1)
    ours(3)
    theirs(5)
    arrived(3)
    scan_states(2)
    scan_states(3)
    theirs(6)
    scan_blocks(2)
    scan_blocks(3)
    for i in range(4, 7):
        ours(i)

    for group_of in by_d + by_z:
        for c in group_of:
            c.wait_send()
    for slot in range(2):
        for f in range(CHUNKS):
            swap(slot, f).wait_send()

    step = wout_hbm.shape[0] // TILES
    hop_cols = wout_hbm.shape[0] // HOPS

    def out_weights(t, g):
        if t == 1:
            return tokg.at[pl.ds(g * step, step)]
        held = onehot if t == 0 else packed.at[t - 2]
        return held.at[pl.ds(0, step), pl.ds(g * group, group)]

    loads = []
    for t in range(TILES):
        for g in range(2):
            loads.append(
                pltpu.make_async_copy(
                    wout_hbm.at[pl.ds(t * step, step), pl.ds(g * group, group)],
                    out_weights(t, g), out_sem.at[t, g],
                )
            )
    for c in loads:
        c.start()

    @pl.when(at_y == 1)
    def _():
        for p in range(4):
            state_copy(p).wait_recv()

    @pl.when(at_y == 0)
    def _():
        arriving[...] = jnp.zeros_like(arriving)

    at_panel = at_x * group + core * share
    where = 2 * at_x + core

    def spread(p, n):
        return remote(
            gated_out.at[block_rows(order[n]), pl.ds(p * 128, 128)],
            whole.at[:, aligned(at_panel + p * 128, 128)],
            g_send.at[p, n], g_recv.at[p, where], 4 * at_y + order[n],
        )

    def arrives(p, source):
        return remote(
            gated_out.at[pl.ds(0, block), pl.ds(0, 128)],
            whole.at[:, aligned(source * share + p * 128, 128)],
            g_send.at[p, 0], g_recv.at[p, source], sibling,
        )

    def sums_to(n):
        return remote(
            sum_sent.at[n], sums.at[where], n_send.at[n], n_recv.at[where], 4 * at_y + order[n]
        )

    def gate(p):
        cols = slice(p * 128, (p + 1) * 128)
        zcols = pl.ds(state + share + p * 128, 128)
        gains = chan_ref[0:1, aligned(at_panel + p * 128, 128)]
        for n, k in enumerate(order):
            if p == 3:
                partials[final][n].wait_recv()
            here, at = block_rows(k), block_ext(k)
            z = (own[at, zcols] + got[at, zcols].astype(f32)).astype(bf).astype(f32)
            held = pair_column(enter_t, p, here) * jnp.dot(
                bc[1, here, :], arriving[p], preferred_element_type=f32
            )
            gated = (ssd[here, cols] + held) * (z / (1.0 + jnp.exp(-z)))
            total = gated * gated
            if p > 0:
                total = total + square[here, :]
            gated_out[here, cols] = (gated * gains).astype(bf)
            if n < 3:
                spread(p, n).start()
            else:
                whole[:, aligned(at_panel + p * 128, 128)] = gated_out[here, cols]
            if p < 3:
                square[here, :] = total
            else:
                sum_sent[n] = jnp.broadcast_to(jnp.sum(total.T, axis=0, keepdims=True), (8, block))
                if n < 3:
                    sums_to(n).start()
                else:
                    sums[where] = sum_sent[n]

    arrived(4)
    gate(0)
    gate(1)
    arrived(5)
    gate(2)
    gate(3)

    for source in order[:3]:
        for p in range(4):
            arrives(p, source).wait_recv()
        remote(
            sum_sent.at[0], sums.at[source], n_send.at[0], n_recv.at[source], sibling
        ).wait_recv()

    scales = []
    for g in range(2):
        total = sums[2 * g, 0:1, :] + sums[2 * g + 1, 0:1, :]
        inv = column(lax.rsqrt(total * (1.0 / group) + 1e-05))
        scales.append(jnp.concatenate([inv, inv], axis=1))

    inner = m * (3 - m) // 2
    end = inner * 3 * (m - 1) + (1 - inner) * m
    near = 1 + end // 3
    away = 3 - near
    opp = 3 - end
    quad = block // 4

    def piece_of(j, t):
        row = (t * hop_cols // step) * block
        return pl.ds(pl.multiple_of(row + j * quad, quad), quad), pl.ds(t * hop_cols % step, hop_cols)

    def hop(i, slot, to, t):
        c = pl.ds(t * hop_cols, hop_cols)
        return along_mp(
            out_sent.at[i, :, c], out_got.at[slot, :, c], o_send.at[i, t], o_recv.at[slot, t], to
        )

    for t in range(HOPS):
        tile = t * hop_cols // step
        if t * hop_cols % step == 0:
            loads[2 * tile].wait()
            loads[2 * tile + 1].wait()
        for u in range(hop_cols // 256):
            at = t * hop_cols % step + u * 256
            sides = [
                lax.dot_general(
                    whole[:, g * group : (g + 1) * group],
                    out_weights(tile, g)[at : at + 256, :],
                    (((1,), (1,)), ((), ())), preferred_element_type=f32,
                )
                for g in range(2)
            ]
            own[tile * block : (tile + 1) * block, at : at + 256] = sides[0] * scales[0] + sides[1] * scales[1]

        c = pl.ds(t * hop_cols, hop_cols)

        @pl.when(inner == 0)
        def _():
            for slot, j in ((2, opp), (1, away), (0, near)):
                out_sent[slot, :, c] = own[piece_of(j, t)].astype(bf)
                hop(slot, slot, near, t).start()

        @pl.when(inner == 1)
        def _():
            out_sent[0, :, c] = own[piece_of(end, t)].astype(bf)
            hop(0, 0, end, t).start()

    @pl.when(inner == 1)
    def _():
        for t in range(HOPS):
            c = pl.ds(t * hop_cols, hop_cols)
            for i, slot, j in ((1, 1, opp), (2, 3, away)):
                held = 2 if i == 1 else 1
                hop(i, held, j, t).wait_recv()
                out_sent[i, :, c] = (
                    own[piece_of(j, t)] + out_got[held, :, c].astype(f32)
                ).astype(bf)
                hop(i, slot, j, t).start()
        for t in range(HOPS):
            c = pl.ds(t * hop_cols, hop_cols)
            hop(0, 0, end, t).wait_recv()
            hop(0, 3, end, t).wait_recv()
            out_ref[:, c] = (
                own[piece_of(m, t)] + out_got[0, :, c].astype(f32) + out_got[3, :, c].astype(f32)
            ).astype(bf)

    @pl.when(inner == 0)
    def _():
        for t in range(HOPS):
            c = pl.ds(t * hop_cols, hop_cols)
            hop(0, 0, near, t).wait_recv()
            hop(0, 1, near, t).wait_recv()
            out_ref[:, c] = (
                own[piece_of(m, t)] + out_got[0, :, c].astype(f32) + out_got[1, :, c].astype(f32)
            ).astype(bf)

    for t in range(HOPS):
        for i in range(3):
            hop(i, 0, near * (1 - inner) + end * inner, t).wait_send()
    for n in range(3):
        for p in range(4):
            spread(p, n).wait_send()
        sums_to(n).wait_send()
    for c in copies + [to_sibling, step_copy, bc_copy] + wsib + wstep:
        c.wait_send()
    for group_of in by_y[0] + by_y[1] + by_x + wfirst + wrest + partials:
        for c in group_of:
            c.wait_send()

    @pl.when(at_y == 0)
    def _():
        for p in range(4):
            state_copy(p).wait_send()


def mix(tokens, source, segment, w_in, w_dt, conv_x, conv_bc, dt_bias, decay, skip, chan, w_out):
    rows, depth = tokens.shape[0], w_in.shape[0]
    width = w_in.shape[1] // 5
    state = width // 4
    share = width // 2
    feats, kdim, span = 2 * depth, 4 * depth, 4 * rows
    ext = span + HALO
    heads = w_dt.shape[0]
    outs = w_out.shape[0]
    f32, bf = jnp.float32, jnp.bfloat16
    vmem = pl.BlockSpec(memory_space=pltpu.VMEM)
    hbm = pl.BlockSpec(memory_space=pl.ANY)
    smem = pl.BlockSpec(memory_space=pltpu.SMEM)
    dma = pltpu.SemaphoreType.DMA

    def buf(shape, kind=f32):
        return pltpu.VMEM(shape, kind)

    return pl.pallas_call(
        mixer_kernel,
        out_shape=jax.ShapeDtypeStruct((rows // 4, outs), bf),
        in_specs=[hbm, vmem, vmem, hbm] + [vmem] * 5 + [smem, vmem, hbm],
        out_specs=vmem,
        scratch_shapes=[
            buf((8, rows), jnp.int32), buf((8, 8, rows), jnp.int32),
            buf((8 * rows, feats), bf), buf((8 * rows + HALO, 128), jnp.int32),
            buf((ext, 8 * rows), bf), buf((2, ext, kdim), bf),
            buf((kdim, 5 * state), bf), buf((4, 16, depth), bf), buf((16, kdim), bf), buf((kdim, 128), bf),
            buf((ext, 5 * state), bf), buf((ext, 5 * state), bf), buf((ext, 5 * state)),
            buf((8, span)), buf((8, span)), buf((8, span)),
            buf((3, ext, 128)), buf((2, span, state), bf), buf((state, span), bf),
            buf((span, share), bf), buf((4, rows, rows)), buf((4, rows, rows)), buf((2, heads, 128)),
            buf((8, span)), buf((8, span)), buf((8, span)), buf((8, span)), buf((8, span)),
            buf((4, 8, 128)), buf((2, 4, state, 128), bf),
            buf((4, state, 128), bf), buf((4, state, 128), bf),
            buf((span, share)), buf((span, share), bf), buf((span, 128)), buf((4, 8, rows)),
            buf((rows, 2 * width), bf), buf((4, 8, rows)),
            buf((3, rows // 4, outs), bf), buf((4, rows // 4, outs), bf),
            dma((2,)), dma((4,)), dma((7,)), dma((7,)),
            dma((4, CHUNKS)), dma((4, CHUNKS)), dma((2, CHUNKS)), dma((2, CHUNKS)),
            dma((2, CHUNKS)), dma((2, CHUNKS)), dma((4, CHUNKS)), dma((4, CHUNKS)),
            dma, dma, dma((3, 7)), dma((3, 7)), dma((2, 4)), dma((2, 4)), dma((10,)), dma((10,)), dma, dma,
            dma((2, CHUNKS)), dma((2, CHUNKS)), dma, dma, dma((4,)), dma((4,)),
            dma((4, 4)), dma((4, 4)), dma((4,)), dma((4,)),
            dma((TILES, 2)), dma((3, HOPS)), dma((4, HOPS)),
        ],
        compiler_params=pltpu.CompilerParams(
            collective_id=0, has_side_effects=True, vmem_limit_bytes=54 << 20
        ),
    )(tokens, source, segment, w_in, w_dt, conv_x, conv_bc, dt_bias, decay, skip, chan, w_out)


def on_plane(
    tokens, pack_source, segment_ids, w_in, w_dt, w_out, conv_x, conv_bc,
    dt_bias, decay_rate, skip_gain, norm_gain,
):
    return mix(
        tokens, pack_source.reshape(1, -1), segment_ids.reshape(1, -1), w_in, w_dt.T, conv_x, conv_bc,
        dt_bias.reshape(1, -1), decay_rate.reshape(1, -1), skip_gain, norm_gain.reshape(1, -1), w_out,
    )


def solution(mesh):
    placed = (
        P("dp", None),
        P("dp"),
        P("dp"),
        P("dp", "mp"),
        P("dp", "mp"),
        P(None, "mp"),
        P(None, "mp"),
        P(None, None, "mp"),
        P("mp"),
        P("mp"),
        P("mp"),
        P("mp"),
    )
    body = on_plane if mesh.shape["dp"] == 8 and mesh.shape["mp"] == 4 else on_device
    return jax.shard_map(
        body, mesh=mesh, in_specs=placed, out_specs=P(("dp", "mp"), None), check_vma=False
    )
```

```python
import jax
import jax.numpy as jnp
from jax import lax
from jax.experimental import pallas as pl
from jax.experimental.pallas import tpu as pltpu
from jax.sharding import PartitionSpec as P

HEAD_DIM = 64
STATE = 256
CONV = 4
BLOCK = 256


highest = lax.Precision.HIGHEST


def passed_along(x, axis, by):
    size = lax.axis_size(axis)
    pairs = [(i, i + by) for i in range(size) if 0 <= i + by < size]
    return lax.ppermute(x, axis, pairs)


def carried_in(x, axis, join, neutral):
    place = lax.axis_index(axis)
    gathered = jax.tree.map(
        lambda a, kind: lax.all_gather(a.astype(kind), axis), x, (jnp.bfloat16, jnp.bfloat16)
    )
    state = jax.tree.map(lambda a, e: jnp.zeros_like(a) + jnp.asarray(e, a.dtype), x, neutral)

    def one(hop, state):
        return join(
            state,
            jax.tree.map(
                lambda a, own: lax.dynamic_index_in_dim(a, hop, 0, False).astype(own.dtype),
                gathered,
                x,
            ),
        )

    return lax.fori_loop(0, place, one, state)


def chain_combine(earlier, later_part):
    return (earlier[0] * later_part[0], later_part[0][:, None, None] * earlier[1] + later_part[1])


def running_sum(values):
    places = jnp.arange(values.shape[0])
    lower = (places[:, None] >= places[None, :]).astype(values.dtype)
    return jnp.dot(lower, values, precision=highest)


def block_step(carry, pieces):
    state_now, prev_seg = carry
    x_block, b_block, c_block, step_dt, step_rate, seg_block = pieces
    per_group = x_block.shape[1] // b_block.shape[1]
    cum_rate = running_sum(step_rate)
    places = jnp.arange(seg_block.shape[0])
    linked = (seg_block[:, None] == seg_block[None, :]) & (places[:, None] >= places[None, :])
    log_spans = cum_rate.T[:, :, None] - cum_rate.T[:, None, :]
    decay_mat = jnp.where(linked[None], jnp.exp(jnp.where(linked[None], log_spans, 0.0)), 0.0)
    scores = jnp.einsum("tgn,sgn->gts", c_block, b_block, preferred_element_type=jnp.float32)
    scores = jnp.repeat(scores, per_group, axis=0)
    mixing = (scores * decay_mat * step_dt.T[:, None, :]).astype(jnp.bfloat16)
    in_block = jnp.einsum("hts,shp->thp", mixing, x_block, preferred_element_type=jnp.float32)
    c_heads = jnp.repeat(c_block.astype(jnp.float32), per_group, axis=1)
    b_heads = jnp.repeat(b_block.astype(jnp.float32), per_group, axis=1)
    entry_mask = jnp.where((seg_block == prev_seg)[:, None], jnp.exp(cum_rate), 0.0)
    from_before = entry_mask[:, :, None] * jnp.einsum(
        "thn,hpn->thp", c_heads, state_now, precision=highest
    )
    last_seg = seg_block[-1]
    weight = (
        jnp.where((seg_block == last_seg)[:, None], jnp.exp(cum_rate[-1][None, :] - cum_rate), 0.0)
        * step_dt
    )
    carried = jnp.where(last_seg == prev_seg, jnp.exp(cum_rate[-1]), 0.0)
    added_in = jnp.einsum(
        "shp,shn->hpn", weight[:, :, None] * x_block.astype(jnp.float32), b_heads, precision=highest
    )
    return ((carried[:, None, None] * state_now + added_in, last_seg), in_block + from_before)


def on_device(
    tokens,
    pack_source,
    segment_ids,
    w_in,
    w_dt,
    w_out,
    conv_x,
    conv_bc,
    dt_bias,
    decay_rate,
    skip_gain,
    norm_gain,
):
    row_count = tokens.shape[0]
    data_devs = lax.axis_size("dp")
    capacity = 2 * row_count // data_devs
    source_dev = pack_source // row_count
    source_row = pack_source % row_count
    same_source = source_dev[:, None] == source_dev[None, :]
    earlier_rows = pack_source[None, :] < pack_source[:, None]
    rank_in = jnp.sum((same_source & earlier_rows).astype(jnp.int32), axis=1)
    slot_index = source_dev * capacity + rank_in
    requests = (
        jnp.full((data_devs * capacity,), -1, jnp.int32)
        .at[slot_index]
        .set(source_row)
        .reshape(data_devs, capacity)
    )
    wanted = lax.all_to_all(requests, "dp", split_axis=0, concat_axis=0, tiled=True)
    fetched = jnp.where(
        (wanted >= 0)[:, :, None], tokens[jnp.maximum(wanted, 0)], jnp.zeros((), jnp.bfloat16)
    )
    replies = lax.all_to_all(fetched, "dp", split_axis=0, concat_axis=0, tiled=True)
    gathered = replies.reshape(data_devs * capacity, tokens.shape[1])[slot_index]
    panel_cols = w_in.shape[1]
    head_count = w_dt.shape[1]
    chan_width = w_out.shape[1]
    proj_sum = jnp.dot(
        gathered, lax.all_gather(w_in, "dp", axis=0, tiled=True), preferred_element_type=jnp.float32
    )
    step_sum = jnp.dot(
        gathered, lax.all_gather(w_dt, "dp", axis=0, tiled=True), preferred_element_type=jnp.float32
    )
    proj_sum, dt_raw = (proj_sum, step_sum)
    projected = proj_sum.astype(jnp.bfloat16)
    group_width = (panel_cols - 2 * chan_width) // 2
    gate_in = projected[:, chan_width : 2 * chan_width]
    stacked = jnp.concatenate([projected[:, :chan_width], projected[:, 2 * chan_width :]], axis=1)
    tail_len = CONV - 1
    tail_vals = stacked[row_count - tail_len :].astype(jnp.float32)
    tail_seg = (segment_ids[row_count - tail_len :] + 1).astype(jnp.float32)
    prev_vals, prev_seg = passed_along((tail_vals, tail_seg), "dp", 1)
    extended = jnp.concatenate([prev_vals.astype(jnp.bfloat16), stacked], axis=0)
    seg_ext = jnp.concatenate([prev_seg.astype(jnp.int32) - 1, segment_ids], axis=0)
    kernel = jnp.concatenate([conv_x, conv_bc.reshape(CONV, 2 * group_width)], axis=1)
    conv_sum = jnp.zeros((row_count, stacked.shape[1]), jnp.float32)
    for lag_index in range(CONV):
        same_seg = (seg_ext[lag_index : lag_index + row_count] == segment_ids)[:, None]
        conv_sum = conv_sum + jnp.where(
            same_seg,
            kernel[lag_index][None, :]
            * extended[lag_index : lag_index + row_count].astype(jnp.float32),
            0.0,
        )
    convolved = jax.nn.silu(conv_sum).astype(jnp.bfloat16)
    local_groups = group_width // STATE
    x_all = convolved[:, :chan_width].reshape(row_count, head_count, HEAD_DIM)
    b_all = convolved[:, chan_width : chan_width + group_width].reshape(
        row_count, local_groups, STATE
    )
    c_all = convolved[:, chan_width + group_width :].reshape(row_count, local_groups, STATE)
    step_dt = jax.nn.softplus(dt_raw + dt_bias)
    step_rate = -step_dt * decay_rate
    seg_before = seg_ext[tail_len - 1]
    block_total = row_count // BLOCK

    def to_blocks(values):
        return values.reshape((block_total, BLOCK) + values.shape[1:])

    start_state = (jnp.zeros((head_count, HEAD_DIM, STATE), jnp.float32), seg_before)
    final, outputs = lax.scan(
        block_step,
        start_state,
        (
            to_blocks(x_all),
            to_blocks(b_all),
            to_blocks(c_all),
            to_blocks(step_dt),
            to_blocks(step_rate),
            to_blocks(segment_ids),
        ),
    )
    local_state = final[0]
    scan_out = outputs.reshape(row_count, head_count, HEAD_DIM)
    running = running_sum(step_rate)
    carry_gain = jnp.where(segment_ids[-1] == seg_before, jnp.exp(running[-1]), 0.0)
    neutral = (jnp.ones((head_count,), jnp.float32), jnp.zeros_like(local_state))
    incoming = carried_in((carry_gain, local_state), "dp", chain_combine, neutral)[1]
    c_heads = jnp.repeat(c_all.astype(jnp.float32), head_count // local_groups, axis=1)
    entry_mask = jnp.where((segment_ids == seg_before)[:, None], jnp.exp(running), 0.0)
    scan_out = scan_out + entry_mask[:, :, None] * jnp.einsum(
        "thn,hpn->thp", c_heads, incoming, precision=highest
    )
    scan_out = scan_out + skip_gain[None, :, None] * x_all.astype(jnp.float32)
    gated_out = scan_out.reshape(row_count, chan_width) * jax.nn.silu(gate_in.astype(jnp.float32))
    grouped = gated_out.reshape(row_count, local_groups, chan_width // local_groups)
    inv_rms = lax.rsqrt(jnp.mean(grouped * grouped, axis=2, keepdims=True) + 1e-05)
    normed = ((grouped * inv_rms).reshape(row_count, chan_width) * norm_gain).astype(jnp.bfloat16)
    return lax.psum_scatter(
        lax.dot_general(
            normed, w_out, (((1,), (1,)), ((), ())), preferred_element_type=jnp.float32
        ).astype(jnp.bfloat16),
        "mp",
        scatter_dimension=0,
        tiled=True,
    )


HALO = 16
CHUNKS = 4
MESH = pl.DeviceIdType.MESH


def remote(src, dst, send, recv, dp):
    return pltpu.make_async_remote_copy(
        src_ref=src, dst_ref=dst, send_sem=send, recv_sem=recv,
        device_id={"dp": dp}, device_id_type=MESH,
    )


def along_mp(src, dst, send, recv, mp):
    return pltpu.make_async_remote_copy(
        src_ref=src, dst_ref=dst, send_sem=send, recv_sem=recv,
        device_id={"mp": mp}, device_id_type=MESH,
    )


def column(row):
    return jnp.broadcast_to(row, (128, row.shape[1])).T


def aligned(start, size):
    return pl.ds(pl.multiple_of(start, 128), size)


TILES = 4
HOPS = 2 * TILES


def mixer_kernel(
    tok_hbm, source_ref, segment_ref, w_hbm, wdt_ref, tapx_ref, tapbc_ref, dtb_ref, decay_ref, skip_ref,
    chan_ref, wout_hbm,
    out_ref,
    meta_ref, metas, tokg, idxcol, onehot, packed, wbuf, wdt_all, wdtt, wdtc, sent, got, own,
    dt_sent, dt_got, dt_own, same, bc, bt, xs, scores, bias, head_cols,
    cum_t, dt_t, w_t, entry_t, enter_t, gain_t, entering, leaving, arriving, ssd, gated_out, square, sum_sent,
    whole, sums, out_sent, out_got,
    loc_sem, wloc_sem, meta_send, meta_recv, y_send, y_recv, x_send, x_recv, d_send, d_recv, z_send, z_recv,
    s_send, s_recv, w_send, w_recv, v_send, v_recv, p_send, p_recv, t_send, t_recv, q_send, q_recv,
    bc_send, bc_recv, st_send, st_recv, g_send, g_recv, n_send, n_recv, out_sem, o_send, o_recv,
):
    f32, bf = jnp.float32, jnp.bfloat16
    me, m = lax.axis_index("dp"), lax.axis_index("mp")
    core = me % 2
    at_x = (me // 2) % 2
    at_y = me // 4
    sibling = me + 1 - 2 * core
    beside = m + 1 - 2 * (m % 2)
    half = m % 2
    x_dev = [4 * at_y + 2 * (1 - at_x) + c for c in (core, 1 - core)]
    y_dev = [4 * (1 - at_y) + 2 * at_x + c for c in (core, 1 - core)]
    d_dev = [4 * (1 - at_y) + 2 * (1 - at_x) + c for c in (core, 1 - core)]
    cores = (core, 1 - core)

    rows, depth = tok_hbm.shape[0], w_hbm.shape[0]
    width = w_hbm.shape[1] // 5
    group, state = width, width // 4
    share = group // 2
    feats = 2 * depth
    kdim = 2 * feats
    span = 4 * rows
    ext = span + HALO
    part = rows // 2
    sizes = (feats // 4, 3 * feats // 8, feats // 4, feats // 8)
    starts = [sum(sizes[:f]) for f in range(CHUNKS)]
    block = rows

    barrier = pltpu.get_barrier_semaphore()
    for k in range(1, 8):
        pl.semaphore_signal(barrier, inc=1, device_id={"dp": (me + k) % 8}, device_id_type=MESH)
    for k in range(1, 4):
        pl.semaphore_signal(barrier, inc=1, device_id={"mp": (m + k) % 4}, device_id_type=MESH)
    meta_ref[...] = jnp.concatenate(
        [source_ref[...], segment_ref[...], jnp.zeros((6, rows), jnp.int32)], axis=0
    )

    pieces = (
        (0, 128), (128, 128), (state, state), (2 * state, state), (3 * state, state),
        (4 * state, 128), (4 * state + 128, 128),
    )
    regions = ((0, state), (state, share), (state + share, share))
    final = len(pieces) - 1

    def of_columns(x, c, col):
        if col < state:
            return 4 * width + c * 2 * state + x * state + col
        if col < state + share:
            return x * group + c * share + col - state
        return 2 * width + x * group + c * share + col - state - share

    for g in range(4):
        wdt_all[g] = jnp.concatenate(
            [wdt_ref[8 * g : 8 * g + 8, :].astype(f32), jnp.zeros((8, depth), f32)], axis=0
        ).astype(bf)
    head_cols[0] = column(dtb_ref[...])
    head_cols[1] = column(decay_ref[...])

    kmine = pl.ds(pl.multiple_of(depth * (2 * at_x + core), depth), depth)
    wlocal = [
        pltpu.make_async_copy(
            w_hbm.at[:, aligned(of_columns(at_x, core, col), size)],
            wbuf.at[kmine, pl.ds(col, size)], wloc_sem.at[i],
        )
        for i, (col, size) in enumerate(regions)
    ]
    wlocal.append(pltpu.make_async_copy(wdt_all.at[2 * at_x + core], wdtt.at[:, kmine], wloc_sem.at[3]))
    mine_rows = pl.ds(pl.multiple_of(me * rows, rows), rows)

    def features(y, c, start, size):
        return aligned(y * kdim + c * feats + start, size)

    local_tok = pltpu.make_async_copy(
        tok_hbm.at[:, features(at_y, core, 0, feats)], tokg.at[mine_rows], loc_sem.at[0]
    )
    local_tok.start()
    for c in wlocal:
        c.start()
    pl.semaphore_wait(barrier, 10)

    copies = []
    for k in range(1, 8):
        copies.append(
            remote(meta_ref, metas.at[me], meta_send.at[k - 1], meta_recv.at[k - 1], (me + k) % 8)
        )
    local_meta = pltpu.make_async_copy(meta_ref, metas.at[me], loc_sem.at[1])
    for c in copies + [local_meta]:
        c.start()

    def half_rows(dev, which):
        return pl.ds(pl.multiple_of(dev * rows + which * part, part), part)

    def fcols(f):
        return pl.ds(starts[f], sizes[f])

    by_y, by_x, by_d, by_z = [[], []], [], [], []
    for f in range(CHUNKS):
        for side, passing in enumerate((half, 1 - half)):
            by_y[side].append([
                remote(
                    tok_hbm.at[pl.ds(pl.multiple_of(passing * part, part), part),
                               features(1 - at_y, cores[r], starts[f], sizes[f])],
                    tokg.at[half_rows(me, passing), fcols(f)],
                    y_send.at[2 * side + r, f], y_recv.at[2 * side + r, f], y_dev[r],
                )
                for r in range(2)
            ])
        by_x.append([
            remote(
                tok_hbm.at[pl.ds(pl.multiple_of(half * part, part), part),
                           features(at_y, cores[r], starts[f], sizes[f])],
                tokg.at[half_rows(me, half), fcols(f)],
                x_send.at[r, f], x_recv.at[r, f], x_dev[r],
            )
            for r in range(2)
        ])
        by_d.append([
            remote(
                tokg.at[half_rows(y_dev[r], half), fcols(f)], tokg.at[half_rows(y_dev[r], half), fcols(f)],
                d_send.at[r, f], d_recv.at[r, f], x_dev[0],
            )
            for r in range(2)
        ])
        by_z.append([
            along_mp(
                tokg.at[half_rows(dev, half), fcols(f)], tokg.at[half_rows(dev, half), fcols(f)],
                z_send.at[i, f], z_recv.at[i, f], beside,
            )
            for i, dev in enumerate(x_dev + d_dev)
        ])
    def begin(group_of):
        for c in group_of:
            c.start()

    begin(by_y[0][0] + by_x[0] + by_y[0][1] + by_x[1] + by_y[0][2] + by_y[0][3])
    for f in range(CHUNKS):
        begin(by_y[1][f])
    to_sibling = remote(
        tok_hbm.at[:, features(at_y, 1 - core, 0, feats)], tokg.at[mine_rows],
        s_send, s_recv, sibling,
    )
    to_sibling.start()
    wsib = [
        remote(
            w_hbm.at[:, aligned(of_columns(at_x, 1 - core, col), size)],
            wbuf.at[kmine, pl.ds(col, size)], w_send.at[0, i], w_recv.at[0, i], sibling,
        )
        for i, (col, size) in enumerate(regions)
    ]
    wsib.append(
        remote(wdt_all.at[2 * at_x + 1 - core], wdtt.at[:, kmine], w_send.at[0, 3], w_recv.at[0, 3], sibling)
    )
    for c in wsib:
        c.start()

    quarter = depth // 4
    wfirst = [
        [
            remote(
                w_hbm.at[pl.ds(q * quarter, quarter), aligned(of_columns(1 - at_x, cores[r], 0), 128)],
                wbuf.at[pl.ds(pl.multiple_of(depth * (2 * at_x + core) + q * quarter, quarter), quarter),
                        pl.ds(0, 128)],
                v_send.at[r, q], v_recv.at[r, q], x_dev[r],
            )
            for r in range(2)
        ]
        for q in range(4)
    ]
    wrest = [
        [
            remote(
                w_hbm.at[:, aligned(of_columns(1 - at_x, cores[r], col), size)],
                wbuf.at[kmine, pl.ds(col, size)],
                w_send.at[1 + r, i], w_recv.at[1 + r, i], x_dev[r],
            )
            for r in range(2)
        ]
        for i, (col, size) in enumerate(pieces) if i > 0
    ]
    wstep = [
        remote(
            wdt_all.at[2 * (1 - at_x) + cores[r]], wdtt.at[:, kmine],
            w_send.at[1 + r, 0], w_recv.at[1 + r, 0], x_dev[r],
        )
        for r in range(2)
    ]

    def index_column():
        for c in copies:
            c.wait_recv()
        local_meta.wait()
        idxcol[0:HALO, :] = jnp.full((HALO, 128), -1, jnp.int32)
        for j in range(8):
            idxcol[HALO + j * rows : HALO + (j + 1) * rows, :] = column(metas[j, 0:1, :])

    lane_row = lax.broadcasted_iota(jnp.int32, (1, 128), 1)

    def choose(which, quarter):
        steps = 8 * rows // 128 // 4

        @pl.loop(quarter * steps, (quarter + 1) * steps)
        def _(t):
            ids = idxcol[pl.ds(pl.multiple_of(which * span, span), ext), :]
            onehot[:, pl.ds(pl.multiple_of(t * 128, 128), 128)] = jnp.where(
                ids == lane_row + t * 128, 1.0, 0.0
            ).astype(bf)

    def place(f):
        return pl.ds(pl.multiple_of(core * feats + starts[f], 128), sizes[f])

    def swap(slot, f):
        there = packed.at[slot, :, place(f)]
        return remote(there, there, q_send.at[slot, f], q_recv.at[slot, f], sibling)

    def pack(slot, f):
        packed[slot, :, place(f)] = jnp.dot(
            onehot[...], tokg[:, fcols(f)], preferred_element_type=f32
        ).astype(bf)
        swap(slot, f).start()


    def y_stage(f):
        for r in range(2):
            by_y[0][f][r].wait_recv()
            by_d[f][r].start()

    def x_stage(f):
        for r in range(2):
            by_x[f][r].wait_recv()
            by_z[f][r].start()

    def d_stage(f):
        for r in range(2):
            by_d[f][r].wait_recv()
            by_z[f][2 + r].start()

    def last_stage(f):
        for c in by_y[1][f] + by_z[f]:
            c.wait_recv()

    x_stage(0)
    y_stage(0)
    begin(by_x[2])
    index_column()
    x_stage(1)
    y_stage(1)
    choose(1 - at_y, 0)
    d_stage(0)
    y_stage(2)
    begin(by_x[3])
    choose(1 - at_y, 1)
    x_stage(2)
    y_stage(3)
    for group_of in wfirst + [wstep] + wrest:
        begin(group_of)
    choose(1 - at_y, 2)
    d_stage(1)
    choose(1 - at_y, 3)
    local_tok.wait()
    to_sibling.wait_recv()
    last_stage(0)
    pack(0, 0)
    d_stage(2)
    last_stage(1)
    x_stage(3)
    pack(0, 1)
    last_stage(2)
    d_stage(3)
    pack(0, 2)
    last_stage(3)
    pack(0, 3)

    order = (2 * (1 - at_x), 2 * (1 - at_x) + 1, 2 * at_x + 1 - core, 2 * at_x + core)

    def block_rows(k):
        return pl.ds(pl.multiple_of(k * block, block), block)

    def block_ext(k):
        return pl.ds(pl.multiple_of(k * block + HALO, HALO), block)

    def product(slot, i):
        col, size = pieces[i]
        return jnp.dot(packed[slot], wbuf[:, pl.ds(col, size)], preferred_element_type=f32)

    def partial(i):
        col, size = pieces[i]
        if i < final:
            at = pl.ds(0, ext) if i < 4 else pl.ds(HALO, span)
            spots = [(at, i)]
        else:
            spots = [(block_ext(k), final + n) for n, k in enumerate(order)]
        return [
            remote(
                sent.at[at, pl.ds(col, size)], got.at[at, pl.ds(col, size)],
                p_send.at[n], p_recv.at[n], y_dev[0],
            )
            for at, n in spots
        ]

    partials = [partial(i) for i in range(len(pieces))]

    def theirs(i):
        if i > 0:
            for c in wrest[i - 1]:
                c.wait_recv()
        sent[:, pl.ds(*pieces[i])] = product(0, i).astype(bf)
        for c in partials[i]:
            c.start()

    def ours(i):
        own[:, pl.ds(*pieces[i])] = product(1, i)

    step_copy = remote(dt_sent, dt_got, t_send, t_recv, y_dev[0])

    for c in wlocal:
        c.wait()
    for c in wsib:
        c.wait_recv()
    for q in range(4):
        for c in wfirst[q]:
            c.wait_recv()

    def half_product(c):
        depths = pl.ds(pl.multiple_of(c * feats, 128), feats)
        return jnp.dot(
            packed[0, :, depths], wbuf[depths, pl.ds(*pieces[0])], preferred_element_type=f32
        )

    first = half_product(core)
    for f in range(CHUNKS):
        swap(0, f).wait_recv()
    sent[:, pl.ds(*pieces[0])] = (first + half_product(1 - core)).astype(bf)
    for c in partials[0]:
        c.start()
    for c in wstep:
        c.wait_recv()
    wdtc[...] = jnp.concatenate(
        [wdtt[...].astype(f32), jnp.zeros((112, kdim), f32)], axis=0
    ).T.astype(bf)
    dt_sent[...] = jnp.dot(packed[0, HALO:, :], wdtc[...], preferred_element_type=f32).T[0:8]
    step_copy.start()
    theirs(1)

    for q in range(4):
        choose(at_y, q)
    for f in range(CHUNKS):
        pack(1, f)

    theirs(2)
    for f in range(CHUNKS):
        swap(1, f).wait_recv()
    ours(0)
    ours(1)
    dt_own[...] = jnp.dot(packed[1, HALO:, :], wdtc[...], preferred_element_type=f32).T[0:8]

    def seg_row(k):
        return metas[4 * at_y + k, 1:2, :]

    earlier = metas[(4 * at_y + 7) % 8, 1:2, :] * at_y - (1 - at_y)
    seg_ext = jnp.concatenate(
        [column(earlier)[rows - HALO :]] + [column(seg_row(k)) for k in range(4)], axis=0
    )
    for k in range(1, CONV):
        same[k - 1] = jnp.where(pltpu.roll(seg_ext, k, 0) == seg_ext, 1.0, 0.0)
    for k in range(4):
        seg_col = column(seg_row(k))
        for t in range(2):
            here = slice(t * 128, (t + 1) * 128)
            linked = (seg_col == seg_row(k)[:, here]) & (
                lax.broadcasted_iota(jnp.int32, (block, 128), 0)
                >= lax.broadcasted_iota(jnp.int32, (block, 128), 1) + t * 128
            )
            bias[k, :, here] = jnp.where(linked, 0.0, -1e30)

    def arrived(i):
        for c in partials[i]:
            c.wait_recv()

    def projected(k, col, size):
        at = pl.ds(k * block, size)
        cols = pl.ds(col, 128)
        return (own[at, cols] + got[at, cols].astype(f32)).astype(bf).astype(f32)

    def convolved(k, col, taps):
        v = projected(k, col, block + HALO)
        total = taps[CONV - 1 : CONV] * v
        for j in range(1, CONV):
            total = total + same[j - 1, pl.ds(k * block, block + HALO), :] * (
                taps[CONV - 1 - j : CONV - j] * pltpu.roll(v, j, 0)
            )
        total = total[HALO:]
        return (total / (1.0 + jnp.exp(-total))).astype(bf)

    arrived(0)
    arrived(1)
    for k in range(4):
        for t in range(state // 128):
            at = pl.ds(pl.multiple_of(at_x * state + t * 128, 128), 128)
            bc[core, pl.ds(k * block, block), t * 128 : (t + 1) * 128] = convolved(
                k, t * 128, jnp.where(core == 0, tapbc_ref[:, 0, at], tapbc_ref[:, 1, at])
            )
    bc_copy = remote(bc.at[core], bc.at[core], bc_send, bc_recv, sibling)
    bc_copy.start()

    step_copy.wait_recv()
    my_heads = pl.ds(pl.multiple_of(8 * (2 * at_x + core), 8), 8)
    bias_col, decay_col = head_cols[0, my_heads, :][:, 0:1], head_cols[1, my_heads, :][:, 0:1]
    u = dt_own[...] + dt_got[...] + bias_col
    step_dt = jnp.maximum(u, 0.0) + jnp.log1p(jnp.exp(-jnp.abs(u)))
    rate = -step_dt * decay_col
    dt_t[...] = step_dt
    upper = jnp.where(
        lax.broadcasted_iota(jnp.int32, (block, block), 0)
        <= lax.broadcasted_iota(jnp.int32, (block, block), 1), 1.0, 0.0
    ).astype(bf)
    before = earlier[:, rows - 1 :]
    first_before = before
    passed = jnp.zeros((8, 1), f32)
    for k in range(4):
        here = slice(k * block, (k + 1) * block)
        r = rate[:, here]
        high = r.astype(bf)
        middle = (r - high.astype(f32)).astype(bf)
        low = (r - high.astype(f32) - middle.astype(f32)).astype(bf)
        three = jnp.dot(
            jnp.concatenate([high.astype(f32), middle.astype(f32), low.astype(f32)], axis=0).astype(bf),
            upper, preferred_element_type=f32,
        )
        cum = three[0:8] + three[8:16] + three[16:24]
        cum_t[:, here] = cum
        last = cum[:, block - 1 :]
        seg = seg_row(k)
        seg_last = seg[:, block - 1 :]
        at_last = jnp.where(seg == seg_last, 1.0, 0.0)
        w_t[:, here] = jnp.exp(last - cum) * step_dt[:, here] * at_last
        entry_t[:, here] = jnp.exp(cum) * jnp.where(seg == before, 1.0, 0.0)
        enter_t[:, here] = jnp.exp(cum + passed) * jnp.where(seg == first_before, 1.0, 0.0)
        keeps = jnp.where(seg_last == before, 1.0, 0.0)
        gain_t[k] = jnp.broadcast_to(jnp.exp(last) * keeps, (8, 128))
        passed = passed + last
        before = seg_last

    theirs(3)
    ours(2)
    bc_copy.wait_recv()
    bt[...] = bc[0].astype(f32).T.astype(bf)
    for k in range(4):
        here = pl.ds(k * block, block)
        scores[k] = jnp.dot(bc[1, here, :], bt[:, here], preferred_element_type=f32)

    lane = lax.broadcasted_iota(jnp.int32, (1, 128), 1)

    def pair_rows(ref, p, here):
        return ref[2 * p : 2 * p + 1, here], ref[2 * p + 1 : 2 * p + 2, here]

    def pair_column(ref, p, here):
        a, b = pair_rows(ref, p, here)
        return jnp.concatenate(
            [jnp.broadcast_to(a, (64, a.shape[1])), jnp.broadcast_to(b, (64, b.shape[1]))], axis=0
        ).T

    def state_copy(p):
        return remote(leaving.at[p], arriving.at[p], st_send.at[p], st_recv.at[p], y_dev[0])

    def scan_states(p):
        cols = slice(p * 128, (p + 1) * 128)
        at = aligned(at_x * group + core * share + p * 128, 128)
        taps = tapx_ref[:, at]
        now = jnp.zeros((state, 128), f32)
        for k in range(4):
            here = slice(k * block, (k + 1) * block)
            x = convolved(k, state + p * 128, taps)
            xs[here, cols] = x
            weighted = (pair_column(w_t, p, here) * x.astype(f32)).astype(bf)
            entering[p % 2, k] = now.astype(bf)
            gain = jnp.where(lane < 64, gain_t[k, 2 * p : 2 * p + 1, :], gain_t[k, 2 * p + 1 : 2 * p + 2, :])
            now = gain * now + jnp.dot(bt[:, here], weighted, preferred_element_type=f32)
        leaving[p] = now.astype(bf)

        @pl.when(at_y == 0)
        def _():
            state_copy(p).start()

    def scan_blocks(p):
        cols = slice(p * 128, (p + 1) * 128)
        at_head = at_x * (group // HEAD_DIM) + core * (share // HEAD_DIM) + 2 * p
        skips = jnp.where(lane < 64, skip_ref[at_head], skip_ref[at_head + 1])
        for k in range(4):
            here = slice(k * block, (k + 1) * block)
            cum_rows, dt_rows = pair_rows(cum_t, p, here), pair_rows(dt_t, p, here)
            cum_cols = [column(r) for r in cum_rows]
            far = pair_column(entry_t, p, here) * jnp.dot(
                bc[1, here, :], entering[p % 2, k], preferred_element_type=f32
            )
            for i in range(2):
                top = i * 128
                w = top + 128
                tall = slice(top, w)
                outs = []
                for n in range(2):
                    spans = jnp.concatenate([cum_cols[n][tall]] * (w // 128), axis=1)
                    spans = spans - cum_rows[n][:, :w] + bias[k, tall, :w]
                    mixing = (scores[k, tall, :w] * jnp.exp(spans) * dt_rows[n][:, :w]).astype(bf)
                    outs.append(
                        jnp.dot(mixing, xs[k * block : k * block + w, cols], preferred_element_type=f32)
                    )
                there = slice(k * block + top, k * block + w)
                ssd[there, cols] = (
                    jnp.where(lane < 64, outs[0], outs[1]) + far[tall]
                    + skips * xs[there, cols].astype(f32)
                )

    arrived(2)
    scan_states(0)
    scan_states(1)
    scan_blocks(0)
    theirs(4)
    scan_blocks(1)
    ours(3)
    theirs(5)
    arrived(3)
    scan_states(2)
    scan_states(3)
    theirs(6)
    scan_blocks(2)
    scan_blocks(3)
    for i in range(4, 7):
        ours(i)

    for group_of in by_d + by_z:
        for c in group_of:
            c.wait_send()
    for slot in range(2):
        for f in range(CHUNKS):
            swap(slot, f).wait_send()

    step = wout_hbm.shape[0] // TILES
    hop_cols = wout_hbm.shape[0] // HOPS

    def out_weights(t, g):
        if t == 1:
            return tokg.at[pl.ds(g * step, step)]
        held = onehot if t == 0 else packed.at[t - 2]
        return held.at[pl.ds(0, step), pl.ds(g * group, group)]

    loads = []
    for t in range(TILES):
        for g in range(2):
            loads.append(
                pltpu.make_async_copy(
                    wout_hbm.at[pl.ds(t * step, step), pl.ds(g * group, group)],
                    out_weights(t, g), out_sem.at[t, g],
                )
            )
    for c in loads:
        c.start()

    @pl.when(at_y == 0)
    def _():
        arriving[...] = jnp.zeros_like(arriving)

    at_panel = at_x * group + core * share
    where = 2 * at_x + core

    def spread(p, n):
        return remote(
            gated_out.at[block_rows(order[n]), pl.ds(p * 128, 128)],
            whole.at[:, aligned(at_panel + p * 128, 128)],
            g_send.at[p, n], g_recv.at[p, where], 4 * at_y + order[n],
        )

    def arrives(p, source):
        return remote(
            gated_out.at[pl.ds(0, block), pl.ds(0, 128)],
            whole.at[:, aligned(source * share + p * 128, 128)],
            g_send.at[p, 0], g_recv.at[p, source], sibling,
        )

    def sums_to(n):
        return remote(
            sum_sent.at[n], sums.at[where], n_send.at[n], n_recv.at[where], 4 * at_y + order[n]
        )

    def gate(p):
        cols = slice(p * 128, (p + 1) * 128)
        zcols = pl.ds(state + share + p * 128, 128)
        gains = chan_ref[0:1, aligned(at_panel + p * 128, 128)]

        @pl.when(at_y == 1)
        def _():
            state_copy(p).wait_recv()

        for n, k in enumerate(order):
            if p == 3:
                partials[final][n].wait_recv()
            here, at = block_rows(k), block_ext(k)
            z = (own[at, zcols] + got[at, zcols].astype(f32)).astype(bf).astype(f32)
            held = pair_column(enter_t, p, here) * jnp.dot(
                bc[1, here, :], arriving[p], preferred_element_type=f32
            )
            gated = (ssd[here, cols] + held) * (z / (1.0 + jnp.exp(-z)))
            total = gated * gated
            if p > 0:
                total = total + square[here, :]
            gated_out[here, cols] = (gated * gains).astype(bf)
            if n < 3:
                spread(p, n).start()
            else:
                whole[:, aligned(at_panel + p * 128, 128)] = gated_out[here, cols]
            if p < 3:
                square[here, :] = total
            else:
                sum_sent[n] = jnp.broadcast_to(jnp.sum(total.T, axis=0, keepdims=True), (8, block))
                if n < 3:
                    sums_to(n).start()
                else:
                    sums[where] = sum_sent[n]

    arrived(4)
    gate(0)
    gate(1)
    arrived(5)
    gate(2)
    gate(3)

    for source in order[:3]:
        for p in range(4):
            arrives(p, source).wait_recv()
        remote(
            sum_sent.at[0], sums.at[source], n_send.at[0], n_recv.at[source], sibling
        ).wait_recv()

    scales = []
    for g in range(2):
        total = sums[2 * g, 0:1, :] + sums[2 * g + 1, 0:1, :]
        inv = column(lax.rsqrt(total * (1.0 / group) + 1e-05))
        scales.append(jnp.concatenate([inv, inv], axis=1))

    inner = m * (3 - m) // 2
    end = inner * 3 * (m - 1) + (1 - inner) * m
    near = 1 + end // 3
    away = 3 - near
    opp = 3 - end
    quad = block // 4

    def piece_of(j, t):
        row = (t * hop_cols // step) * block
        return pl.ds(pl.multiple_of(row + j * quad, quad), quad), pl.ds(t * hop_cols % step, hop_cols)

    def hop(i, slot, to, t):
        c = pl.ds(t * hop_cols, hop_cols)
        return along_mp(
            out_sent.at[i, :, c], out_got.at[slot, :, c], o_send.at[i, t], o_recv.at[slot, t], to
        )

    for t in range(HOPS):
        tile = t * hop_cols // step
        if t * hop_cols % step == 0:
            loads[2 * tile].wait()
            loads[2 * tile + 1].wait()
        for u in range(hop_cols // 256):
            at = t * hop_cols % step + u * 256
            sides = [
                lax.dot_general(
                    whole[:, g * group : (g + 1) * group],
                    out_weights(tile, g)[at : at + 256, :],
                    (((1,), (1,)), ((), ())), preferred_element_type=f32,
                )
                for g in range(2)
            ]
            own[tile * block : (tile + 1) * block, at : at + 256] = sides[0] * scales[0] + sides[1] * scales[1]

        c = pl.ds(t * hop_cols, hop_cols)

        @pl.when(inner == 0)
        def _():
            for slot, j in ((2, opp), (1, away), (0, near)):
                out_sent[slot, :, c] = own[piece_of(j, t)].astype(bf)
                hop(slot, slot, near, t).start()

        @pl.when(inner == 1)
        def _():
            out_sent[0, :, c] = own[piece_of(end, t)].astype(bf)
            hop(0, 0, end, t).start()

    @pl.when(inner == 1)
    def _():
        for t in range(HOPS):
            c = pl.ds(t * hop_cols, hop_cols)
            for i, slot, j in ((1, 1, opp), (2, 3, away)):
                held = 2 if i == 1 else 1
                hop(i, held, j, t).wait_recv()
                out_sent[i, :, c] = (
                    own[piece_of(j, t)] + out_got[held, :, c].astype(f32)
                ).astype(bf)
                hop(i, slot, j, t).start()
        for t in range(HOPS):
            c = pl.ds(t * hop_cols, hop_cols)
            hop(0, 0, end, t).wait_recv()
            hop(0, 3, end, t).wait_recv()
            out_ref[:, c] = (
                own[piece_of(m, t)] + out_got[0, :, c].astype(f32) + out_got[3, :, c].astype(f32)
            ).astype(bf)

    @pl.when(inner == 0)
    def _():
        for t in range(HOPS):
            c = pl.ds(t * hop_cols, hop_cols)
            hop(0, 0, near, t).wait_recv()
            hop(0, 1, near, t).wait_recv()
            out_ref[:, c] = (
                own[piece_of(m, t)] + out_got[0, :, c].astype(f32) + out_got[1, :, c].astype(f32)
            ).astype(bf)

    for t in range(HOPS):
        for i in range(3):
            hop(i, 0, near * (1 - inner) + end * inner, t).wait_send()
    for n in range(3):
        for p in range(4):
            spread(p, n).wait_send()
        sums_to(n).wait_send()
    for c in copies + [to_sibling, step_copy, bc_copy] + wsib + wstep:
        c.wait_send()
    for group_of in by_y[0] + by_y[1] + by_x + wfirst + wrest + partials:
        for c in group_of:
            c.wait_send()

    @pl.when(at_y == 0)
    def _():
        for p in range(4):
            state_copy(p).wait_send()


def mix(tokens, source, segment, w_in, w_dt, conv_x, conv_bc, dt_bias, decay, skip, chan, w_out):
    rows, depth = tokens.shape[0], w_in.shape[0]
    width = w_in.shape[1] // 5
    state = width // 4
    share = width // 2
    feats, kdim, span = 2 * depth, 4 * depth, 4 * rows
    ext = span + HALO
    heads = w_dt.shape[0]
    outs = w_out.shape[0]
    f32, bf = jnp.float32, jnp.bfloat16
    vmem = pl.BlockSpec(memory_space=pltpu.VMEM)
    hbm = pl.BlockSpec(memory_space=pl.ANY)
    smem = pl.BlockSpec(memory_space=pltpu.SMEM)
    dma = pltpu.SemaphoreType.DMA

    def buf(shape, kind=f32):
        return pltpu.VMEM(shape, kind)

    return pl.pallas_call(
        mixer_kernel,
        out_shape=jax.ShapeDtypeStruct((rows // 4, outs), bf),
        in_specs=[hbm, vmem, vmem, hbm] + [vmem] * 5 + [smem, vmem, hbm],
        out_specs=vmem,
        scratch_shapes=[
            buf((8, rows), jnp.int32), buf((8, 8, rows), jnp.int32),
            buf((8 * rows, feats), bf), buf((8 * rows + HALO, 128), jnp.int32),
            buf((ext, 8 * rows), bf), buf((2, ext, kdim), bf),
            buf((kdim, 5 * state), bf), buf((4, 16, depth), bf), buf((16, kdim), bf), buf((kdim, 128), bf),
            buf((ext, 5 * state), bf), buf((ext, 5 * state), bf), buf((ext, 5 * state)),
            buf((8, span)), buf((8, span)), buf((8, span)),
            buf((3, ext, 128)), buf((2, span, state), bf), buf((state, span), bf),
            buf((span, share), bf), buf((4, rows, rows)), buf((4, rows, rows)), buf((2, heads, 128)),
            buf((8, span)), buf((8, span)), buf((8, span)), buf((8, span)), buf((8, span)),
            buf((4, 8, 128)), buf((2, 4, state, 128), bf),
            buf((4, state, 128), bf), buf((4, state, 128), bf),
            buf((span, share)), buf((span, share), bf), buf((span, 128)), buf((4, 8, rows)),
            buf((rows, 2 * width), bf), buf((4, 8, rows)),
            buf((3, rows // 4, outs), bf), buf((4, rows // 4, outs), bf),
            dma((2,)), dma((4,)), dma((7,)), dma((7,)),
            dma((4, CHUNKS)), dma((4, CHUNKS)), dma((2, CHUNKS)), dma((2, CHUNKS)),
            dma((2, CHUNKS)), dma((2, CHUNKS)), dma((4, CHUNKS)), dma((4, CHUNKS)),
            dma, dma, dma((3, 7)), dma((3, 7)), dma((2, 4)), dma((2, 4)), dma((10,)), dma((10,)), dma, dma,
            dma((2, CHUNKS)), dma((2, CHUNKS)), dma, dma, dma((4,)), dma((4,)),
            dma((4, 4)), dma((4, 4)), dma((4,)), dma((4,)),
            dma((TILES, 2)), dma((3, HOPS)), dma((4, HOPS)),
        ],
        compiler_params=pltpu.CompilerParams(
            collective_id=0, has_side_effects=True, vmem_limit_bytes=54 << 20
        ),
    )(tokens, source, segment, w_in, w_dt, conv_x, conv_bc, dt_bias, decay, skip, chan, w_out)


def on_plane(
    tokens, pack_source, segment_ids, w_in, w_dt, w_out, conv_x, conv_bc,
    dt_bias, decay_rate, skip_gain, norm_gain,
):
    return mix(
        tokens, pack_source.reshape(1, -1), segment_ids.reshape(1, -1), w_in, w_dt.T, conv_x, conv_bc,
        dt_bias.reshape(1, -1), decay_rate.reshape(1, -1), skip_gain, norm_gain.reshape(1, -1), w_out,
    )


def solution(mesh):
    placed = (
        P("dp", None),
        P("dp"),
        P("dp"),
        P("dp", "mp"),
        P("dp", "mp"),
        P(None, "mp"),
        P(None, "mp"),
        P(None, None, "mp"),
        P("mp"),
        P("mp"),
        P("mp"),
        P("mp"),
    )
    body = on_plane if mesh.shape["dp"] == 8 and mesh.shape["mp"] == 4 else on_device
    return jax.shard_map(
        body, mesh=mesh, in_specs=placed, out_specs=P(("dp", "mp"), None), check_vma=False
    )
```

```python
import jax
import jax.numpy as jnp
from jax import lax
from jax.experimental import pallas as pl
from jax.experimental.pallas import tpu as pltpu
from jax.sharding import PartitionSpec as P

HEAD_DIM = 64
STATE = 256
CONV = 4
BLOCK = 256


highest = lax.Precision.HIGHEST


def passed_along(x, axis, by):
    size = lax.axis_size(axis)
    pairs = [(i, i + by) for i in range(size) if 0 <= i + by < size]
    return lax.ppermute(x, axis, pairs)


def carried_in(x, axis, join, neutral):
    place = lax.axis_index(axis)
    gathered = jax.tree.map(
        lambda a, kind: lax.all_gather(a.astype(kind), axis), x, (jnp.bfloat16, jnp.bfloat16)
    )
    state = jax.tree.map(lambda a, e: jnp.zeros_like(a) + jnp.asarray(e, a.dtype), x, neutral)

    def one(hop, state):
        return join(
            state,
            jax.tree.map(
                lambda a, own: lax.dynamic_index_in_dim(a, hop, 0, False).astype(own.dtype),
                gathered,
                x,
            ),
        )

    return lax.fori_loop(0, place, one, state)


def chain_combine(earlier, later_part):
    return (earlier[0] * later_part[0], later_part[0][:, None, None] * earlier[1] + later_part[1])


def running_sum(values):
    places = jnp.arange(values.shape[0])
    lower = (places[:, None] >= places[None, :]).astype(values.dtype)
    return jnp.dot(lower, values, precision=highest)


def block_step(carry, pieces):
    state_now, prev_seg = carry
    x_block, b_block, c_block, step_dt, step_rate, seg_block = pieces
    per_group = x_block.shape[1] // b_block.shape[1]
    cum_rate = running_sum(step_rate)
    places = jnp.arange(seg_block.shape[0])
    linked = (seg_block[:, None] == seg_block[None, :]) & (places[:, None] >= places[None, :])
    log_spans = cum_rate.T[:, :, None] - cum_rate.T[:, None, :]
    decay_mat = jnp.where(linked[None], jnp.exp(jnp.where(linked[None], log_spans, 0.0)), 0.0)
    scores = jnp.einsum("tgn,sgn->gts", c_block, b_block, preferred_element_type=jnp.float32)
    scores = jnp.repeat(scores, per_group, axis=0)
    mixing = (scores * decay_mat * step_dt.T[:, None, :]).astype(jnp.bfloat16)
    in_block = jnp.einsum("hts,shp->thp", mixing, x_block, preferred_element_type=jnp.float32)
    c_heads = jnp.repeat(c_block.astype(jnp.float32), per_group, axis=1)
    b_heads = jnp.repeat(b_block.astype(jnp.float32), per_group, axis=1)
    entry_mask = jnp.where((seg_block == prev_seg)[:, None], jnp.exp(cum_rate), 0.0)
    from_before = entry_mask[:, :, None] * jnp.einsum(
        "thn,hpn->thp", c_heads, state_now, precision=highest
    )
    last_seg = seg_block[-1]
    weight = (
        jnp.where((seg_block == last_seg)[:, None], jnp.exp(cum_rate[-1][None, :] - cum_rate), 0.0)
        * step_dt
    )
    carried = jnp.where(last_seg == prev_seg, jnp.exp(cum_rate[-1]), 0.0)
    added_in = jnp.einsum(
        "shp,shn->hpn", weight[:, :, None] * x_block.astype(jnp.float32), b_heads, precision=highest
    )
    return ((carried[:, None, None] * state_now + added_in, last_seg), in_block + from_before)


def on_device(
    tokens,
    pack_source,
    segment_ids,
    w_in,
    w_dt,
    w_out,
    conv_x,
    conv_bc,
    dt_bias,
    decay_rate,
    skip_gain,
    norm_gain,
):
    row_count = tokens.shape[0]
    data_devs = lax.axis_size("dp")
    capacity = 2 * row_count // data_devs
    source_dev = pack_source // row_count
    source_row = pack_source % row_count
    same_source = source_dev[:, None] == source_dev[None, :]
    earlier_rows = pack_source[None, :] < pack_source[:, None]
    rank_in = jnp.sum((same_source & earlier_rows).astype(jnp.int32), axis=1)
    slot_index = source_dev * capacity + rank_in
    requests = (
        jnp.full((data_devs * capacity,), -1, jnp.int32)
        .at[slot_index]
        .set(source_row)
        .reshape(data_devs, capacity)
    )
    wanted = lax.all_to_all(requests, "dp", split_axis=0, concat_axis=0, tiled=True)
    fetched = jnp.where(
        (wanted >= 0)[:, :, None], tokens[jnp.maximum(wanted, 0)], jnp.zeros((), jnp.bfloat16)
    )
    replies = lax.all_to_all(fetched, "dp", split_axis=0, concat_axis=0, tiled=True)
    gathered = replies.reshape(data_devs * capacity, tokens.shape[1])[slot_index]
    panel_cols = w_in.shape[1]
    head_count = w_dt.shape[1]
    chan_width = w_out.shape[1]
    proj_sum = jnp.dot(
        gathered, lax.all_gather(w_in, "dp", axis=0, tiled=True), preferred_element_type=jnp.float32
    )
    step_sum = jnp.dot(
        gathered, lax.all_gather(w_dt, "dp", axis=0, tiled=True), preferred_element_type=jnp.float32
    )
    proj_sum, dt_raw = (proj_sum, step_sum)
    projected = proj_sum.astype(jnp.bfloat16)
    group_width = (panel_cols - 2 * chan_width) // 2
    gate_in = projected[:, chan_width : 2 * chan_width]
    stacked = jnp.concatenate([projected[:, :chan_width], projected[:, 2 * chan_width :]], axis=1)
    tail_len = CONV - 1
    tail_vals = stacked[row_count - tail_len :].astype(jnp.float32)
    tail_seg = (segment_ids[row_count - tail_len :] + 1).astype(jnp.float32)
    prev_vals, prev_seg = passed_along((tail_vals, tail_seg), "dp", 1)
    extended = jnp.concatenate([prev_vals.astype(jnp.bfloat16), stacked], axis=0)
    seg_ext = jnp.concatenate([prev_seg.astype(jnp.int32) - 1, segment_ids], axis=0)
    kernel = jnp.concatenate([conv_x, conv_bc.reshape(CONV, 2 * group_width)], axis=1)
    conv_sum = jnp.zeros((row_count, stacked.shape[1]), jnp.float32)
    for lag_index in range(CONV):
        same_seg = (seg_ext[lag_index : lag_index + row_count] == segment_ids)[:, None]
        conv_sum = conv_sum + jnp.where(
            same_seg,
            kernel[lag_index][None, :]
            * extended[lag_index : lag_index + row_count].astype(jnp.float32),
            0.0,
        )
    convolved = jax.nn.silu(conv_sum).astype(jnp.bfloat16)
    local_groups = group_width // STATE
    x_all = convolved[:, :chan_width].reshape(row_count, head_count, HEAD_DIM)
    b_all = convolved[:, chan_width : chan_width + group_width].reshape(
        row_count, local_groups, STATE
    )
    c_all = convolved[:, chan_width + group_width :].reshape(row_count, local_groups, STATE)
    step_dt = jax.nn.softplus(dt_raw + dt_bias)
    step_rate = -step_dt * decay_rate
    seg_before = seg_ext[tail_len - 1]
    block_total = row_count // BLOCK

    def to_blocks(values):
        return values.reshape((block_total, BLOCK) + values.shape[1:])

    start_state = (jnp.zeros((head_count, HEAD_DIM, STATE), jnp.float32), seg_before)
    final, outputs = lax.scan(
        block_step,
        start_state,
        (
            to_blocks(x_all),
            to_blocks(b_all),
            to_blocks(c_all),
            to_blocks(step_dt),
            to_blocks(step_rate),
            to_blocks(segment_ids),
        ),
    )
    local_state = final[0]
    scan_out = outputs.reshape(row_count, head_count, HEAD_DIM)
    running = running_sum(step_rate)
    carry_gain = jnp.where(segment_ids[-1] == seg_before, jnp.exp(running[-1]), 0.0)
    neutral = (jnp.ones((head_count,), jnp.float32), jnp.zeros_like(local_state))
    incoming = carried_in((carry_gain, local_state), "dp", chain_combine, neutral)[1]
    c_heads = jnp.repeat(c_all.astype(jnp.float32), head_count // local_groups, axis=1)
    entry_mask = jnp.where((segment_ids == seg_before)[:, None], jnp.exp(running), 0.0)
    scan_out = scan_out + entry_mask[:, :, None] * jnp.einsum(
        "thn,hpn->thp", c_heads, incoming, precision=highest
    )
    scan_out = scan_out + skip_gain[None, :, None] * x_all.astype(jnp.float32)
    gated_out = scan_out.reshape(row_count, chan_width) * jax.nn.silu(gate_in.astype(jnp.float32))
    grouped = gated_out.reshape(row_count, local_groups, chan_width // local_groups)
    inv_rms = lax.rsqrt(jnp.mean(grouped * grouped, axis=2, keepdims=True) + 1e-05)
    normed = ((grouped * inv_rms).reshape(row_count, chan_width) * norm_gain).astype(jnp.bfloat16)
    return lax.psum_scatter(
        lax.dot_general(
            normed, w_out, (((1,), (1,)), ((), ())), preferred_element_type=jnp.float32
        ).astype(jnp.bfloat16),
        "mp",
        scatter_dimension=0,
        tiled=True,
    )


HALO = 16
CHUNKS = 4
MESH = pl.DeviceIdType.MESH


def remote(src, dst, send, recv, dp):
    return pltpu.make_async_remote_copy(
        src_ref=src, dst_ref=dst, send_sem=send, recv_sem=recv,
        device_id={"dp": dp}, device_id_type=MESH,
    )


def along_mp(src, dst, send, recv, mp):
    return pltpu.make_async_remote_copy(
        src_ref=src, dst_ref=dst, send_sem=send, recv_sem=recv,
        device_id={"mp": mp}, device_id_type=MESH,
    )


def column(row):
    return jnp.broadcast_to(row, (128, row.shape[1])).T


def aligned(start, size):
    return pl.ds(pl.multiple_of(start, 128), size)


TILES = 4
HOPS = 2 * TILES


def mixer_kernel(
    tok_hbm, source_ref, segment_ref, w_hbm, wdt_ref, tapx_ref, tapbc_ref, dtb_ref, decay_ref, skip_ref,
    chan_ref, wout_hbm,
    out_ref,
    meta_ref, metas, tokg, idxcol, onehot, packed, wbuf, wdt_all, wdtt, wdtc, sent, got, own,
    dt_sent, dt_got, dt_own, same, bc, bt, xs, scores, bias, head_cols,
    cum_t, dt_t, w_t, entry_t, enter_t, gain_t, entering, leaving, arriving, ssd, gated_out, square, sum_sent,
    whole, sums, out_sent, out_got,
    loc_sem, wloc_sem, meta_send, meta_recv, y_send, y_recv, x_send, x_recv, d_send, d_recv, z_send, z_recv,
    s_send, s_recv, w_send, w_recv, v_send, v_recv, p_send, p_recv, t_send, t_recv, q_send, q_recv,
    bc_send, bc_recv, st_send, st_recv, g_send, g_recv, n_send, n_recv, out_sem, o_send, o_recv,
):
    f32, bf = jnp.float32, jnp.bfloat16
    me, m = lax.axis_index("dp"), lax.axis_index("mp")
    core = me % 2
    at_x = (me // 2) % 2
    at_y = me // 4
    sibling = me + 1 - 2 * core
    beside = m + 1 - 2 * (m % 2)
    half = m % 2
    x_dev = [4 * at_y + 2 * (1 - at_x) + c for c in (core, 1 - core)]
    y_dev = [4 * (1 - at_y) + 2 * at_x + c for c in (core, 1 - core)]
    d_dev = [4 * (1 - at_y) + 2 * (1 - at_x) + c for c in (core, 1 - core)]
    cores = (core, 1 - core)

    rows, depth = tok_hbm.shape[0], w_hbm.shape[0]
    width = w_hbm.shape[1] // 5
    group, state = width, width // 4
    share = group // 2
    feats = 2 * depth
    kdim = 2 * feats
    span = 4 * rows
    ext = span + HALO
    part = rows // 2
    sizes = (feats // 4, 3 * feats // 8, feats // 4, feats // 8)
    starts = [sum(sizes[:f]) for f in range(CHUNKS)]
    block = rows

    barrier = pltpu.get_barrier_semaphore()
    for k in range(1, 8):
        pl.semaphore_signal(barrier, inc=1, device_id={"dp": (me + k) % 8}, device_id_type=MESH)
    for k in range(1, 4):
        pl.semaphore_signal(barrier, inc=1, device_id={"mp": (m + k) % 4}, device_id_type=MESH)
    meta_ref[...] = jnp.concatenate(
        [source_ref[...], segment_ref[...], jnp.zeros((6, rows), jnp.int32)], axis=0
    )

    pieces = (
        (0, 128), (128, 128), (state, state), (2 * state, state), (3 * state, state),
        (4 * state, 128), (4 * state + 128, 128),
    )
    regions = ((0, state), (state, share), (state + share, share))
    final = len(pieces) - 1

    def of_columns(x, c, col):
        if col < state:
            return 4 * width + c * 2 * state + x * state + col
        if col < state + share:
            return x * group + c * share + col - state
        return 2 * width + x * group + c * share + col - state - share

    for g in range(4):
        wdt_all[g] = jnp.concatenate(
            [wdt_ref[8 * g : 8 * g + 8, :].astype(f32), jnp.zeros((8, depth), f32)], axis=0
        ).astype(bf)
    head_cols[0] = column(dtb_ref[...])
    head_cols[1] = column(decay_ref[...])

    kmine = pl.ds(pl.multiple_of(depth * (2 * at_x + core), depth), depth)
    wlocal = [
        pltpu.make_async_copy(
            w_hbm.at[:, aligned(of_columns(at_x, core, col), size)],
            wbuf.at[kmine, pl.ds(col, size)], wloc_sem.at[i],
        )
        for i, (col, size) in enumerate(regions)
    ]
    wlocal.append(pltpu.make_async_copy(wdt_all.at[2 * at_x + core], wdtt.at[:, kmine], wloc_sem.at[3]))
    mine_rows = pl.ds(pl.multiple_of(me * rows, rows), rows)

    def features(y, c, start, size):
        return aligned(y * kdim + c * feats + start, size)

    local_tok = pltpu.make_async_copy(
        tok_hbm.at[:, features(at_y, core, 0, feats)], tokg.at[mine_rows], loc_sem.at[0]
    )
    local_tok.start()
    for c in wlocal:
        c.start()
    pl.semaphore_wait(barrier, 10)

    copies = []
    for k in range(1, 8):
        copies.append(
            remote(meta_ref, metas.at[me], meta_send.at[k - 1], meta_recv.at[k - 1], (me + k) % 8)
        )
    local_meta = pltpu.make_async_copy(meta_ref, metas.at[me], loc_sem.at[1])
    for c in copies + [local_meta]:
        c.start()

    def half_rows(dev, which):
        return pl.ds(pl.multiple_of(dev * rows + which * part, part), part)

    def fcols(f):
        return pl.ds(starts[f], sizes[f])

    by_y, by_x, by_d, by_z = [[], []], [], [], []
    for f in range(CHUNKS):
        for side, passing in enumerate((half, 1 - half)):
            by_y[side].append([
                remote(
                    tok_hbm.at[pl.ds(pl.multiple_of(passing * part, part), part),
                               features(1 - at_y, cores[r], starts[f], sizes[f])],
                    tokg.at[half_rows(me, passing), fcols(f)],
                    y_send.at[2 * side + r, f], y_recv.at[2 * side + r, f], y_dev[r],
                )
                for r in range(2)
            ])
        by_x.append([
            remote(
                tok_hbm.at[pl.ds(pl.multiple_of(half * part, part), part),
                           features(at_y, cores[r], starts[f], sizes[f])],
                tokg.at[half_rows(me, half), fcols(f)],
                x_send.at[r, f], x_recv.at[r, f], x_dev[r],
            )
            for r in range(2)
        ])
        by_d.append([
            remote(
                tokg.at[half_rows(y_dev[r], half), fcols(f)], tokg.at[half_rows(y_dev[r], half), fcols(f)],
                d_send.at[r, f], d_recv.at[r, f], x_dev[0],
            )
            for r in range(2)
        ])
        by_z.append([
            along_mp(
                tokg.at[half_rows(dev, half), fcols(f)], tokg.at[half_rows(dev, half), fcols(f)],
                z_send.at[i, f], z_recv.at[i, f], beside,
            )
            for i, dev in enumerate(x_dev + d_dev)
        ])
    def begin(group_of):
        for c in group_of:
            c.start()

    begin(by_y[0][0] + by_x[0] + by_y[0][1] + by_x[1] + by_y[0][2] + by_y[0][3])
    for f in range(CHUNKS):
        begin(by_y[1][f])
    to_sibling = remote(
        tok_hbm.at[:, features(at_y, 1 - core, 0, feats)], tokg.at[mine_rows],
        s_send, s_recv, sibling,
    )
    to_sibling.start()
    wsib = [
        remote(
            w_hbm.at[:, aligned(of_columns(at_x, 1 - core, col), size)],
            wbuf.at[kmine, pl.ds(col, size)], w_send.at[0, i], w_recv.at[0, i], sibling,
        )
        for i, (col, size) in enumerate(regions)
    ]
    wsib.append(
        remote(wdt_all.at[2 * at_x + 1 - core], wdtt.at[:, kmine], w_send.at[0, 3], w_recv.at[0, 3], sibling)
    )
    for c in wsib:
        c.start()

    quarter = depth // 4
    wfirst = [
        [
            remote(
                w_hbm.at[pl.ds(q * quarter, quarter), aligned(of_columns(1 - at_x, cores[r], 0), 128)],
                wbuf.at[pl.ds(pl.multiple_of(depth * (2 * at_x + core) + q * quarter, quarter), quarter),
                        pl.ds(0, 128)],
                v_send.at[r, q], v_recv.at[r, q], x_dev[r],
            )
            for r in range(2)
        ]
        for q in range(4)
    ]
    wrest = [
        [
            remote(
                w_hbm.at[:, aligned(of_columns(1 - at_x, cores[r], col), size)],
                wbuf.at[kmine, pl.ds(col, size)],
                w_send.at[1 + r, i], w_recv.at[1 + r, i], x_dev[r],
            )
            for r in range(2)
        ]
        for i, (col, size) in enumerate(pieces) if i > 0
    ]
    wstep = [
        remote(
            wdt_all.at[2 * (1 - at_x) + cores[r]], wdtt.at[:, kmine],
            w_send.at[1 + r, 0], w_recv.at[1 + r, 0], x_dev[r],
        )
        for r in range(2)
    ]

    def index_column():
        for c in copies:
            c.wait_recv()
        local_meta.wait()
        idxcol[0:HALO, :] = jnp.full((HALO, 128), -1, jnp.int32)
        for j in range(8):
            idxcol[HALO + j * rows : HALO + (j + 1) * rows, :] = column(metas[j, 0:1, :])

    lane_row = lax.broadcasted_iota(jnp.int32, (1, 128), 1)

    def choose(which, quarter):
        steps = 8 * rows // 128 // 4

        @pl.loop(quarter * steps, (quarter + 1) * steps)
        def _(t):
            ids = idxcol[pl.ds(pl.multiple_of(which * span, span), ext), :]
            onehot[:, pl.ds(pl.multiple_of(t * 128, 128), 128)] = jnp.where(
                ids == lane_row + t * 128, 1.0, 0.0
            ).astype(bf)

    def place(f):
        return pl.ds(pl.multiple_of(core * feats + starts[f], 128), sizes[f])

    def swap(slot, f):
        there = packed.at[slot, :, place(f)]
        return remote(there, there, q_send.at[slot, f], q_recv.at[slot, f], sibling)

    def pack(slot, f):
        packed[slot, :, place(f)] = jnp.dot(
            onehot[...], tokg[:, fcols(f)], preferred_element_type=f32
        ).astype(bf)
        swap(slot, f).start()


    def y_stage(f):
        for r in range(2):
            by_y[0][f][r].wait_recv()
            by_d[f][r].start()

    def x_stage(f):
        for r in range(2):
            by_x[f][r].wait_recv()
            by_z[f][r].start()

    def d_stage(f):
        for r in range(2):
            by_d[f][r].wait_recv()
            by_z[f][2 + r].start()

    def last_stage(f):
        for c in by_y[1][f] + by_z[f]:
            c.wait_recv()

    x_stage(0)
    y_stage(0)
    begin(by_x[2])
    index_column()
    x_stage(1)
    y_stage(1)
    choose(1 - at_y, 0)
    d_stage(0)
    y_stage(2)
    begin(by_x[3])
    choose(1 - at_y, 1)
    x_stage(2)
    y_stage(3)
    for group_of in wfirst + [wstep] + wrest:
        begin(group_of)
    choose(1 - at_y, 2)
    d_stage(1)
    choose(1 - at_y, 3)
    local_tok.wait()
    to_sibling.wait_recv()
    last_stage(0)
    pack(0, 0)
    d_stage(2)
    last_stage(1)
    x_stage(3)
    pack(0, 1)
    last_stage(2)
    d_stage(3)
    pack(0, 2)
    last_stage(3)
    pack(0, 3)

    order = (2 * (1 - at_x), 2 * (1 - at_x) + 1, 2 * at_x + 1 - core, 2 * at_x + core)

    def block_rows(k):
        return pl.ds(pl.multiple_of(k * block, block), block)

    def block_ext(k):
        return pl.ds(pl.multiple_of(k * block + HALO, HALO), block)

    def product(slot, i):
        col, size = pieces[i]
        return jnp.dot(packed[slot], wbuf[:, pl.ds(col, size)], preferred_element_type=f32)

    def partial(i):
        col, size = pieces[i]
        if i < final:
            at = pl.ds(0, ext) if i < 4 else pl.ds(HALO, span)
            spots = [(at, i)]
        else:
            spots = [(block_ext(k), final + n) for n, k in enumerate(order)]
        return [
            remote(
                sent.at[at, pl.ds(col, size)], got.at[at, pl.ds(col, size)],
                p_send.at[n], p_recv.at[n], y_dev[0],
            )
            for at, n in spots
        ]

    partials = [partial(i) for i in range(len(pieces))]

    def theirs(i):
        if i > 0:
            for c in wrest[i - 1]:
                c.wait_recv()
        sent[:, pl.ds(*pieces[i])] = product(0, i).astype(bf)
        for c in partials[i]:
            c.start()

    def ours(i):
        own[:, pl.ds(*pieces[i])] = product(1, i)

    step_copy = remote(dt_sent, dt_got, t_send, t_recv, y_dev[0])

    for c in wlocal:
        c.wait()
    for c in wsib:
        c.wait_recv()
    for q in range(4):
        for c in wfirst[q]:
            c.wait_recv()

    def half_product(c):
        depths = pl.ds(pl.multiple_of(c * feats, 128), feats)
        return jnp.dot(
            packed[0, :, depths], wbuf[depths, pl.ds(*pieces[0])], preferred_element_type=f32
        )

    first = half_product(core)
    for f in range(CHUNKS):
        swap(0, f).wait_recv()
    sent[:, pl.ds(*pieces[0])] = (first + half_product(1 - core)).astype(bf)
    for c in partials[0]:
        c.start()
    for c in wstep:
        c.wait_recv()
    wdtc[...] = jnp.concatenate(
        [wdtt[...].astype(f32), jnp.zeros((112, kdim), f32)], axis=0
    ).T.astype(bf)
    dt_sent[...] = jnp.dot(packed[0, HALO:, :], wdtc[...], preferred_element_type=f32).T[0:8]
    step_copy.start()
    theirs(1)

    for q in range(4):
        choose(at_y, q)
    for f in range(CHUNKS):
        pack(1, f)

    theirs(2)
    for f in range(CHUNKS):
        swap(1, f).wait_recv()
    ours(0)
    ours(1)
    dt_own[...] = jnp.dot(packed[1, HALO:, :], wdtc[...], preferred_element_type=f32).T[0:8]

    def seg_row(k):
        return metas[4 * at_y + k, 1:2, :]

    earlier = metas[(4 * at_y + 7) % 8, 1:2, :] * at_y - (1 - at_y)
    seg_ext = jnp.concatenate(
        [column(earlier)[rows - HALO :]] + [column(seg_row(k)) for k in range(4)], axis=0
    )
    for k in range(1, CONV):
        same[k - 1] = jnp.where(pltpu.roll(seg_ext, k, 0) == seg_ext, 1.0, 0.0)
    for k in range(4):
        seg_col = column(seg_row(k))
        for t in range(2):
            here = slice(t * 128, (t + 1) * 128)
            linked = (seg_col == seg_row(k)[:, here]) & (
                lax.broadcasted_iota(jnp.int32, (block, 128), 0)
                >= lax.broadcasted_iota(jnp.int32, (block, 128), 1) + t * 128
            )
            bias[k, :, here] = jnp.where(linked, 0.0, -1e30)

    def arrived(i):
        for c in partials[i]:
            c.wait_recv()

    def projected(k, col, size):
        at = pl.ds(k * block, size)
        cols = pl.ds(col, 128)
        return (own[at, cols] + got[at, cols].astype(f32)).astype(bf).astype(f32)

    def convolved(k, col, taps):
        v = projected(k, col, block + HALO)
        total = taps[CONV - 1 : CONV] * v
        for j in range(1, CONV):
            total = total + same[j - 1, pl.ds(k * block, block + HALO), :] * (
                taps[CONV - 1 - j : CONV - j] * pltpu.roll(v, j, 0)
            )
        total = total[HALO:]
        return (total / (1.0 + jnp.exp(-total))).astype(bf)

    arrived(0)
    arrived(1)
    for k in range(4):
        for t in range(state // 128):
            at = pl.ds(pl.multiple_of(at_x * state + t * 128, 128), 128)
            bc[core, pl.ds(k * block, block), t * 128 : (t + 1) * 128] = convolved(
                k, t * 128, jnp.where(core == 0, tapbc_ref[:, 0, at], tapbc_ref[:, 1, at])
            )
    bc_copy = remote(bc.at[core], bc.at[core], bc_send, bc_recv, sibling)
    bc_copy.start()

    step_copy.wait_recv()
    my_heads = pl.ds(pl.multiple_of(8 * (2 * at_x + core), 8), 8)
    bias_col, decay_col = head_cols[0, my_heads, :][:, 0:1], head_cols[1, my_heads, :][:, 0:1]
    u = dt_own[...] + dt_got[...] + bias_col
    step_dt = jnp.maximum(u, 0.0) + jnp.log1p(jnp.exp(-jnp.abs(u)))
    rate = -step_dt * decay_col
    dt_t[...] = step_dt
    upper = jnp.where(
        lax.broadcasted_iota(jnp.int32, (block, block), 0)
        <= lax.broadcasted_iota(jnp.int32, (block, block), 1), 1.0, 0.0
    ).astype(bf)
    before = earlier[:, rows - 1 :]
    first_before = before
    passed = jnp.zeros((8, 1), f32)
    for k in range(4):
        here = slice(k * block, (k + 1) * block)
        r = rate[:, here]
        high = r.astype(bf)
        middle = (r - high.astype(f32)).astype(bf)
        low = (r - high.astype(f32) - middle.astype(f32)).astype(bf)
        three = jnp.dot(
            jnp.concatenate([high.astype(f32), middle.astype(f32), low.astype(f32)], axis=0).astype(bf),
            upper, preferred_element_type=f32,
        )
        cum = three[0:8] + three[8:16] + three[16:24]
        cum_t[:, here] = cum
        last = cum[:, block - 1 :]
        seg = seg_row(k)
        seg_last = seg[:, block - 1 :]
        at_last = jnp.where(seg == seg_last, 1.0, 0.0)
        w_t[:, here] = jnp.exp(last - cum) * step_dt[:, here] * at_last
        entry_t[:, here] = jnp.exp(cum) * jnp.where(seg == before, 1.0, 0.0)
        enter_t[:, here] = jnp.exp(cum + passed) * jnp.where(seg == first_before, 1.0, 0.0)
        keeps = jnp.where(seg_last == before, 1.0, 0.0)
        gain_t[k] = jnp.broadcast_to(jnp.exp(last) * keeps, (8, 128))
        passed = passed + last
        before = seg_last

    theirs(3)
    ours(2)
    bc_copy.wait_recv()
    bt[...] = bc[0].astype(f32).T.astype(bf)
    for k in range(4):
        here = pl.ds(k * block, block)
        scores[k] = jnp.dot(bc[1, here, :], bt[:, here], preferred_element_type=f32)

    lane = lax.broadcasted_iota(jnp.int32, (1, 128), 1)

    def pair_rows(ref, p, here):
        return ref[2 * p : 2 * p + 1, here], ref[2 * p + 1 : 2 * p + 2, here]

    def pair_column(ref, p, here):
        a, b = pair_rows(ref, p, here)
        return jnp.concatenate(
            [jnp.broadcast_to(a, (64, a.shape[1])), jnp.broadcast_to(b, (64, b.shape[1]))], axis=0
        ).T

    def state_copy(p):
        return remote(leaving.at[p], arriving.at[p], st_send.at[p], st_recv.at[p], y_dev[0])

    def scan_states(p):
        cols = slice(p * 128, (p + 1) * 128)
        at = aligned(at_x * group + core * share + p * 128, 128)
        taps = tapx_ref[:, at]
        now = jnp.zeros((state, 128), f32)
        for k in range(4):
            here = slice(k * block, (k + 1) * block)
            x = convolved(k, state + p * 128, taps)
            xs[here, cols] = x
            weighted = (pair_column(w_t, p, here) * x.astype(f32)).astype(bf)
            entering[p % 2, k] = now.astype(bf)
            gain = jnp.where(lane < 64, gain_t[k, 2 * p : 2 * p + 1, :], gain_t[k, 2 * p + 1 : 2 * p + 2, :])
            now = gain * now + jnp.dot(bt[:, here], weighted, preferred_element_type=f32)
        leaving[p] = now.astype(bf)

        @pl.when(at_y == 0)
        def _():
            state_copy(p).start()

    def scan_blocks(p):
        cols = slice(p * 128, (p + 1) * 128)
        at_head = at_x * (group // HEAD_DIM) + core * (share // HEAD_DIM) + 2 * p
        skips = jnp.where(lane < 64, skip_ref[at_head], skip_ref[at_head + 1])
        for k in range(4):
            here = slice(k * block, (k + 1) * block)
            cum_rows, dt_rows = pair_rows(cum_t, p, here), pair_rows(dt_t, p, here)
            cum_cols = [column(r) for r in cum_rows]
            far = pair_column(entry_t, p, here) * jnp.dot(
                bc[1, here, :], entering[p % 2, k], preferred_element_type=f32
            )
            for i in range(2):
                top = i * 128
                w = top + 128
                tall = slice(top, w)
                outs = []
                for n in range(2):
                    spans = jnp.concatenate([cum_cols[n][tall]] * (w // 128), axis=1)
                    spans = spans - cum_rows[n][:, :w] + bias[k, tall, :w]
                    mixing = (scores[k, tall, :w] * jnp.exp(spans) * dt_rows[n][:, :w]).astype(bf)
                    outs.append(
                        jnp.dot(mixing, xs[k * block : k * block + w, cols], preferred_element_type=f32)
                    )
                there = slice(k * block + top, k * block + w)
                ssd[there, cols] = (
                    jnp.where(lane < 64, outs[0], outs[1]) + far[tall]
                    + skips * xs[there, cols].astype(f32)
                )

    arrived(2)
    scan_states(0)
    scan_states(1)
    scan_blocks(0)
    theirs(4)
    scan_blocks(1)
    ours(3)
    theirs(5)
    arrived(3)
    scan_states(2)
    scan_states(3)
    theirs(6)
    scan_blocks(2)
    scan_blocks(3)
    for i in range(4, 7):
        ours(i)

    for group_of in by_d + by_z:
        for c in group_of:
            c.wait_send()
    for slot in range(2):
        for f in range(CHUNKS):
            swap(slot, f).wait_send()

    step = wout_hbm.shape[0] // TILES
    hop_cols = wout_hbm.shape[0] // HOPS

    def out_weights(t, g):
        if t == 1:
            return tokg.at[pl.ds(g * step, step)]
        held = onehot if t == 0 else packed.at[t - 2]
        return held.at[pl.ds(0, step), pl.ds(g * group, group)]

    loads = []
    for t in range(TILES):
        for g in range(2):
            loads.append(
                pltpu.make_async_copy(
                    wout_hbm.at[pl.ds(t * step, step), pl.ds(g * group, group)],
                    out_weights(t, g), out_sem.at[t, g],
                )
            )
    for c in loads:
        c.start()

    @pl.when(at_y == 0)
    def _():
        arriving[...] = jnp.zeros_like(arriving)

    at_panel = at_x * group + core * share
    where = 2 * at_x + core

    def spread(p, n):
        return remote(
            gated_out.at[block_rows(order[n]), pl.ds(p * 128, 128)],
            whole.at[:, aligned(at_panel + p * 128, 128)],
            g_send.at[p, n], g_recv.at[p, where], 4 * at_y + order[n],
        )

    def arrives(p, source):
        return remote(
            gated_out.at[pl.ds(0, block), pl.ds(0, 128)],
            whole.at[:, aligned(source * share + p * 128, 128)],
            g_send.at[p, 0], g_recv.at[p, source], sibling,
        )

    def sums_to(n):
        return remote(
            sum_sent.at[n], sums.at[where], n_send.at[n], n_recv.at[where], 4 * at_y + order[n]
        )

    def gate(p):
        cols = slice(p * 128, (p + 1) * 128)
        zcols = pl.ds(state + share + p * 128, 128)
        gains = chan_ref[0:1, aligned(at_panel + p * 128, 128)]

        @pl.when(at_y == 1)
        def _():
            state_copy(p).wait_recv()

        for n, k in enumerate(order):
            if p == 3:
                partials[final][n].wait_recv()
            here, at = block_rows(k), block_ext(k)
            z = (own[at, zcols] + got[at, zcols].astype(f32)).astype(bf).astype(f32)
            held = pair_column(enter_t, p, here) * jnp.dot(
                bc[1, here, :], arriving[p], preferred_element_type=f32
            )
            gated = (ssd[here, cols] + held) * (z / (1.0 + jnp.exp(-z)))
            total = gated * gated
            if p > 0:
                total = total + square[here, :]
            gated_out[here, cols] = (gated * gains).astype(bf)
            if n < 3:
                spread(p, n).start()
            else:
                whole[:, aligned(at_panel + p * 128, 128)] = gated_out[here, cols]
            if p < 3:
                square[here, :] = total
            else:
                sum_sent[n] = jnp.broadcast_to(jnp.sum(total.T, axis=0, keepdims=True), (8, block))
                if n < 3:
                    sums_to(n).start()
                else:
                    sums[where] = sum_sent[n]

    arrived(4)
    gate(0)
    gate(1)
    arrived(5)
    gate(2)
    gate(3)

    for source in order[:3]:
        for p in range(4):
            arrives(p, source).wait_recv()
        remote(
            sum_sent.at[0], sums.at[source], n_send.at[0], n_recv.at[source], sibling
        ).wait_recv()

    scales = []
    for g in range(2):
        total = sums[2 * g, 0:1, :] + sums[2 * g + 1, 0:1, :]
        inv = column(lax.rsqrt(total * (1.0 / group) + 1e-05))
        scales.append(jnp.concatenate([inv, inv], axis=1))

    inner = m * (3 - m) // 2
    end = inner * 3 * (m - 1) + (1 - inner) * m
    near = 1 + end // 3
    away = 3 - near
    opp = 3 - end
    quad = block // 4

    def piece_of(j, t):
        row = (t * hop_cols // step) * block
        return pl.ds(pl.multiple_of(row + j * quad, quad), quad), pl.ds(t * hop_cols % step, hop_cols)

    def hop(i, slot, to, t):
        c = pl.ds(t * hop_cols, hop_cols)
        return along_mp(
            out_sent.at[i, :, c], out_got.at[slot, :, c], o_send.at[i, t], o_recv.at[slot, t], to
        )

    for t in range(HOPS):
        tile = t * hop_cols // step
        if t * hop_cols % step == 0:
            loads[2 * tile].wait()
            loads[2 * tile + 1].wait()
        for u in range(hop_cols // 256):
            at = t * hop_cols % step + u * 256
            sides = [
                lax.dot_general(
                    whole[:, g * group : (g + 1) * group],
                    out_weights(tile, g)[at : at + 256, :],
                    (((1,), (1,)), ((), ())), preferred_element_type=f32,
                )
                for g in range(2)
            ]
            own[tile * block : (tile + 1) * block, at : at + 256] = sides[0] * scales[0] + sides[1] * scales[1]

        c = pl.ds(t * hop_cols, hop_cols)

        @pl.when(inner == 0)
        def _():
            for slot, j in ((2, opp), (1, away), (0, near)):
                out_sent[slot, :, c] = own[piece_of(j, t)].astype(bf)
                hop(slot, slot, near, t).start()

        @pl.when(inner == 1)
        def _():
            out_sent[0, :, c] = own[piece_of(end, t)].astype(bf)
            hop(0, 0, end, t).start()

    @pl.when(inner == 1)
    def _():
        for t in range(HOPS):
            c = pl.ds(t * hop_cols, hop_cols)
            for i, slot, j in ((1, 1, opp), (2, 3, away)):
                held = 2 if i == 1 else 1
                hop(i, held, j, t).wait_recv()
                out_sent[i, :, c] = (
                    own[piece_of(j, t)] + out_got[held, :, c].astype(f32)
                ).astype(bf)
                hop(i, slot, j, t).start()
        for t in range(HOPS):
            c = pl.ds(t * hop_cols, hop_cols)
            hop(0, 0, end, t).wait_recv()
            hop(0, 3, end, t).wait_recv()
            out_ref[:, c] = (
                own[piece_of(m, t)] + out_got[0, :, c].astype(f32) + out_got[3, :, c].astype(f32)
            ).astype(bf)

    @pl.when(inner == 0)
    def _():
        for t in range(HOPS):
            c = pl.ds(t * hop_cols, hop_cols)
            hop(0, 0, near, t).wait_recv()
            hop(0, 1, near, t).wait_recv()
            out_ref[:, c] = (
                own[piece_of(m, t)] + out_got[0, :, c].astype(f32) + out_got[1, :, c].astype(f32)
            ).astype(bf)

    for t in range(HOPS):
        for i in range(3):
            hop(i, 0, near * (1 - inner) + end * inner, t).wait_send()
    for n in range(3):
        for p in range(4):
            spread(p, n).wait_send()
        sums_to(n).wait_send()
    for c in copies + [to_sibling, step_copy, bc_copy] + wsib + wstep:
        c.wait_send()
    for group_of in by_y[0] + by_y[1] + by_x + wfirst + wrest + partials:
        for c in group_of:
            c.wait_send()

    @pl.when(at_y == 0)
    def _():
        for p in range(4):
            state_copy(p).wait_send()


def mix(tokens, source, segment, w_in, w_dt, conv_x, conv_bc, dt_bias, decay, skip, chan, w_out):
    rows, depth = tokens.shape[0], w_in.shape[0]
    width = w_in.shape[1] // 5
    state = width // 4
    share = width // 2
    feats, kdim, span = 2 * depth, 4 * depth, 4 * rows
    ext = span + HALO
    heads = w_dt.shape[0]
    outs = w_out.shape[0]
    f32, bf = jnp.float32, jnp.bfloat16
    vmem = pl.BlockSpec(memory_space=pltpu.VMEM)
    hbm = pl.BlockSpec(memory_space=pl.ANY)
    smem = pl.BlockSpec(memory_space=pltpu.SMEM)
    dma = pltpu.SemaphoreType.DMA

    def buf(shape, kind=f32):
        return pltpu.VMEM(shape, kind)

    return pl.pallas_call(
        mixer_kernel,
        out_shape=pltpu.VMEM((rows // 4, outs), bf),
        in_specs=[hbm, vmem, vmem, hbm] + [vmem] * 5 + [smem, vmem, hbm],
        out_specs=vmem,
        scratch_shapes=[
            buf((8, rows), jnp.int32), buf((8, 8, rows), jnp.int32),
            buf((8 * rows, feats), bf), buf((8 * rows + HALO, 128), jnp.int32),
            buf((ext, 8 * rows), bf), buf((2, ext, kdim), bf),
            buf((kdim, 5 * state), bf), buf((4, 16, depth), bf), buf((16, kdim), bf), buf((kdim, 128), bf),
            buf((ext, 5 * state), bf), buf((ext, 5 * state), bf), buf((ext, 5 * state)),
            buf((8, span)), buf((8, span)), buf((8, span)),
            buf((3, ext, 128)), buf((2, span, state), bf), buf((state, span), bf),
            buf((span, share), bf), buf((4, rows, rows)), buf((4, rows, rows)), buf((2, heads, 128)),
            buf((8, span)), buf((8, span)), buf((8, span)), buf((8, span)), buf((8, span)),
            buf((4, 8, 128)), buf((2, 4, state, 128), bf),
            buf((4, state, 128), bf), buf((4, state, 128), bf),
            buf((span, share)), buf((span, share), bf), buf((span, 128)), buf((4, 8, rows)),
            buf((rows, 2 * width), bf), buf((4, 8, rows)),
            buf((3, rows // 4, outs), bf), buf((4, rows // 4, outs), bf),
            dma((2,)), dma((4,)), dma((7,)), dma((7,)),
            dma((4, CHUNKS)), dma((4, CHUNKS)), dma((2, CHUNKS)), dma((2, CHUNKS)),
            dma((2, CHUNKS)), dma((2, CHUNKS)), dma((4, CHUNKS)), dma((4, CHUNKS)),
            dma, dma, dma((3, 7)), dma((3, 7)), dma((2, 4)), dma((2, 4)), dma((10,)), dma((10,)), dma, dma,
            dma((2, CHUNKS)), dma((2, CHUNKS)), dma, dma, dma((4,)), dma((4,)),
            dma((4, 4)), dma((4, 4)), dma((4,)), dma((4,)),
            dma((TILES, 2)), dma((3, HOPS)), dma((4, HOPS)),
        ],
        compiler_params=pltpu.CompilerParams(
            collective_id=0, has_side_effects=True, vmem_limit_bytes=54 << 20
        ),
    )(tokens, source, segment, w_in, w_dt, conv_x, conv_bc, dt_bias, decay, skip, chan, w_out)


def on_plane(
    tokens, pack_source, segment_ids, w_in, w_dt, w_out, conv_x, conv_bc,
    dt_bias, decay_rate, skip_gain, norm_gain,
):
    return mix(
        tokens, pack_source.reshape(1, -1), segment_ids.reshape(1, -1), w_in, w_dt.T, conv_x, conv_bc,
        dt_bias.reshape(1, -1), decay_rate.reshape(1, -1), skip_gain, norm_gain.reshape(1, -1), w_out,
    )


def solution(mesh):
    placed = (
        P("dp", None),
        P("dp"),
        P("dp"),
        P("dp", "mp"),
        P("dp", "mp"),
        P(None, "mp"),
        P(None, "mp"),
        P(None, None, "mp"),
        P("mp"),
        P("mp"),
        P("mp"),
        P("mp"),
    )
    body = on_plane if mesh.shape["dp"] == 8 and mesh.shape["mp"] == 4 else on_device
    return jax.shard_map(
        body, mesh=mesh, in_specs=placed, out_specs=P(("dp", "mp"), None), check_vma=False
    )
```
